32 devices in a mesh: band: 8 (over y, x, core), slab: 4 (over z).
Axes of the slice: x: 2, y: 2, z: 4, core: 2. Of those that a mesh axis runs over, the one named last changes fastest.
Arguments:
- orbitals: float32 [16, 144, 5184], P('band', 'slab'), may hold values from -6 to 6
Outputs:
- exchange: float32 [16, 144, 5184], P('band', 'slab')
The draws below stay inside these ranges and needn't reach their ends.
All inputs are finite; a program needn't handle non-finite values.
Results may differ from the reference program's by a relative error of at most 0.0001.
Values sent between devices are 32-bit elements; how exact they have to be, the bound alone decides.
No kernel may reach another device: no remote copies, remote signals or barrier semaphores. Data moves between devices by JAX's collectives and lax.ppermute only.
A program may use at most 384 MiB of HBM per device.

```python
import jax
import jax.numpy as jnp
from jax import lax

NX = 72
NY = 72
NXY = 5184
NZ = 144
ORB_DEV = 2
ORBS = 16
SWEEPS = 3
CYCLE = 2
N_BAND = 8


def block_levels(own_key, dims, shards, least, top_value):
    def one(position, parts):
        heights = jax.random.uniform(jax.random.fold_in(jax.random.fold_in(own_key, 6), position), (parts,), jnp.float32, least / len(shards), top_value / len(shards))
        return jnp.repeat(jnp.exp(heights), dims[position] // parts).reshape((-1,) + (1,) * (len(dims) - position - 1))

    factor_of = one(*shards[0])
    for cut in shards[1:]:
        factor_of = factor_of * one(*cut)
    return factor_of


def gaussian(stream_key, extent, scale, bound, shards=(), dtype=jnp.bfloat16):
    values = jax.random.normal(stream_key, extent, jnp.float32) * scale
    if len(shards) > 0:
        values = block_levels(stream_key, extent, shards, -0.22, 0.18) * values
    return jnp.clip(values, min=-bound, max=bound).astype(dtype)


def setup_inputs(seed: int = 0) -> dict:
    arg_keys = jax.random.split(jax.random.key(seed), 2)
    orbitals = gaussian(arg_keys[0], (ORBS, NZ, NXY), 1.0, 6.0, ((0, 8), (1, 4)), jnp.float32)
    return dict(orbitals=orbitals)


centre_weight = 8.5


def along_x(field, step):
    return jnp.roll(field, -step * NY, axis=-1)


def along_y(field, step):
    column = jnp.arange(field.shape[-1]) % NY
    inside = jnp.roll(field, -step, axis=-1)
    if step > 0:
        wrapped = jnp.roll(field, NY - step, axis=-1)
        keep = column + step < NY
    else:
        wrapped = jnp.roll(field, -step - NY, axis=-1)
        keep = column + step >= 0
    return jnp.where(keep, inside, wrapped)


def plane_off(field):
    xpart = 16.0 * (along_x(field, -1) + along_x(field, 1)) - (along_x(field, -2) + along_x(field, 2))
    ypart = 16.0 * (along_y(field, -1) + along_y(field, 1)) - (along_y(field, -2) + along_y(field, 2))
    return xpart + ypart


def off_periodic(field):
    zpart = 16.0 * (jnp.roll(field, 1, axis=-2) + jnp.roll(field, -1, axis=-2)) - (jnp.roll(field, 2, axis=-2) + jnp.roll(field, -2, axis=-2))
    return (plane_off(field) + zpart) / 12.0


def potential(density):
    field = density / centre_weight
    for sweep in range(SWEEPS - 1):
        field = (density + off_periodic(field)) / centre_weight
    return field


def reference(orbitals):
    blocks = orbitals.reshape(N_BAND, ORB_DEV, NZ, NX * NY)

    def over_block(index, out):
        index = jnp.asarray(index).astype(jnp.int32)
        own = lax.dynamic_index_in_dim(blocks, index, 0, False)
        for step in range(1, CYCLE + 1):
            other = ((index - step) % N_BAND).astype(jnp.int32)
            partner = lax.dynamic_index_in_dim(blocks, other, 0, False)

            def one(orbit, carry):
                orbit = jnp.asarray(orbit).astype(jnp.int32)
                total, travel = carry
                first = lax.dynamic_index_in_dim(own, orbit, 0, True)
                field = potential(first * partner)
                row = -jnp.sum(field * partner, axis=0, keepdims=True)
                total = lax.dynamic_update_index_in_dim(total, lax.dynamic_index_in_dim(total, orbit, 0, True) + row, orbit, 0)
                return total, travel - field * first

            empty = jnp.zeros((ORB_DEV, NZ, NX * NY), jnp.float32)
            total, travel = lax.fori_loop(0, ORB_DEV, one, (empty, empty))
            out = lax.dynamic_update_index_in_dim(out, lax.dynamic_index_in_dim(out, index, 0, False) + total, index, 0)
            out = lax.dynamic_update_index_in_dim(out, lax.dynamic_index_in_dim(out, other, 0, False) + travel, other, 0)
        return out

    start = jnp.zeros((N_BAND, ORB_DEV, NZ, NX * NY), jnp.float32)
    out = lax.fori_loop(0, N_BAND, over_block, start)
    return out.reshape(ORBS, NZ, NX * NY)
```

```python
import functools

import jax
import jax.numpy as jnp
from jax import lax
from jax.experimental import pallas as pl
from jax.experimental.pallas import tpu as pltpu
from jax.sharding import PartitionSpec as P

NY = 72
LANES = 128
REACH = 2
HALO = 4
CENTRE = 8.5
ALPHA = 1.0 / (12.0 * CENTRE)
VMEM = pl.BlockSpec(memory_space=pltpu.VMEM)
SMEM = pl.BlockSpec(memory_space=pltpu.SMEM)


def params(limit=None):
    return pltpu.CompilerParams(vmem_limit_bytes=limit)


def sds(*shape):
    return jax.ShapeDtypeStruct(shape, jnp.float32)


def call(body, out, inputs, scratch=(), flops=0, smem=False, limit=None, name=None):
    nbytes = sum(4 * x.size for x in inputs) + sum(4 * o.size for o in out)
    specs = [VMEM] * len(inputs)
    if smem:
        specs[0] = SMEM
    return pl.pallas_call(
        body,
        out_shape=out,
        in_specs=specs,
        out_specs=[VMEM] * len(out),
        scratch_shapes=scratch,
        compiler_params=params(limit),
        cost_estimate=pl.CostEstimate(flops=flops, bytes_accessed=nbytes, transcendentals=0),
        name=name,
    )(*inputs)


def pack_body(chips, width, n_in, *refs):
    chip_ref, ins, outs = refs[0], refs[1 : 1 + n_in], refs[1 + n_in :]
    chip = chip_ref[0]
    total = ins[0].shape[2]
    span = (width + 2 * HALO) * NY
    for ahead in range(chips):
        for target in range(chips):

            @pl.when(lax.rem(chip + ahead, chips) == target)
            def _(ahead=ahead, target=target):
                start = (target * width - HALO) * NY
                row = 0
                for ref in ins:
                    rows = ref.shape[1]
                    for orb in range(ref.shape[0]):
                        lo, hi = start, start + span
                        if lo < 0:
                            value = jnp.concatenate(
                                [ref[orb, :, lo + total : total], ref[orb, :, 0:hi]], axis=-1
                            )
                        elif hi > total:
                            value = jnp.concatenate(
                                [ref[orb, :, lo:total], ref[orb, :, 0 : hi - total]], axis=-1
                            )
                        else:
                            value = ref[orb, :, lo:hi]
                        outs[ahead][orb, row : row + rows, :] = value
                    row += rows


def pack(chip, pieces, chips, width):
    orbs = pieces[0].shape[0]
    rows = sum(p.shape[1] for p in pieces)
    span = (width + 2 * HALO) * NY
    return call(
        functools.partial(pack_body, chips, width, len(pieces)),
        [sds(orbs, rows, span)] * chips,
        [chip, *pieces],
        smem=True,
        name="pack",
    )


def gather_body(chips, *refs):
    main, edge, out = refs[:chips], refs[chips : 2 * chips], refs[2 * chips]
    orbs, depth, span = main[0].shape

    def move(sources, lo, hi, at):
        for a in range(0, span, LANES):
            b = min(a + LANES, span)
            value = jnp.concatenate([ref[:, lo:hi, a:b] for ref in sources], axis=0)
            out[at : at + hi - lo, :, a:b] = jnp.swapaxes(value, 0, 1)

    move(edge, 0, HALO, 0)
    for z in range(0, depth, 8):
        move(main, z, min(z + 8, depth), HALO + z)
    move(edge, HALO, 2 * HALO, HALO + depth)


def gather(main, edge):
    orbs, depth, span = main[0].shape
    chips = len(main)
    return call(
        functools.partial(gather_body, chips),
        [sds(depth + 2 * HALO, orbs * chips, span)],
        [*main, *edge],
        name="gather",
    )[0]


def lane_iota(rows):
    return lax.broadcasted_iota(jnp.int32, (rows, LANES), 1)


def row_iota(rows):
    return lax.broadcasted_iota(jnp.int32, (rows, LANES), 0)


def roll_rows(value, shift):
    return pltpu.roll(value, shift % value.shape[0], 0)


def roll_lanes(value, shift):
    return pltpu.roll(value, shift % LANES, 1)


def unpack(flat_ref, out_ref, change=None):
    depth, rows, span = flat_ref.shape
    lane = lane_iota(rows)

    def plane(z, _):
        for col in range(span // NY):
            tile, offset = divmod(col * NY, LANES)
            tile *= LANES
            end = min(tile + LANES, span)
            head = flat_ref[z, :, tile:end]
            if end - tile < LANES:
                head = jnp.concatenate(
                    [head, jnp.zeros((rows, LANES - (end - tile)), jnp.float32)], axis=-1
                )
            value = roll_lanes(head, -offset) if offset else head
            if offset + NY > LANES:
                stop = min(tile + 2 * LANES, span)
                tail = flat_ref[z, :, tile + LANES : stop]
                if stop - tile - LANES < LANES:
                    pad = 2 * LANES - (stop - tile)
                    tail = jnp.concatenate(
                        [tail, jnp.zeros((rows, pad), jnp.float32)], axis=-1
                    )
                value = jnp.where(lane < LANES - offset, value, roll_lanes(tail, -offset))
            if change is not None:
                value = change(value)
            after = roll_lanes(value, NY)
            before = roll_lanes(value, LANES - NY)
            value = jnp.where(
                lane < NY,
                value,
                jnp.where(
                    lane < NY + HALO, after, jnp.where(lane >= LANES - HALO, before, 0.0)
                ),
            )
            out_ref[z, col] = value
        return 0

    lax.fori_loop(0, depth, plane, 0)


def repack(tiles, out_ref, z):
    rows = tiles[0].shape[0]
    lane = lane_iota(rows)
    span = len(tiles) * NY
    for start in range(0, span, LANES):
        stop = min(start + LANES, span)
        value = None
        for col in range(start // NY, (stop - 1) // NY + 1):
            shift = col * NY - start
            part = roll_lanes(tiles[col], shift)
            if value is None:
                value = part
            else:
                value = jnp.where(lane < shift, value, part)
        out_ref[z, :, start:stop] = value[:, : stop - start]


def stencil(source, z, col, centre):
    c = col + REACH
    near = (centre[c - 1] + centre[c + 1]) + (source[z + 1, c] + source[z + 3, c])
    near = near + (roll_lanes(centre[c], 1) + roll_lanes(centre[c], -1))
    far = (centre[c - 2] + centre[c + 2]) + (source[z, c] + source[z + 4, c])
    far = far + (roll_lanes(centre[c], 2) + roll_lanes(centre[c], -2))
    return 16.0 * near - far


def potentials(first, partner, rho, field, finish):
    depth, cols = rho.shape[:2]

    def density(z, _):
        for col in range(cols):
            rho[z, col] = first[z, col] * partner[z, col]
        return 0

    lax.fori_loop(0, depth, density, 0)

    def sweep(z, _):
        centre = [rho[z + REACH, col] for col in range(cols)]
        for col in range(cols - 2 * REACH):
            field[z, col] = centre[col + REACH] + ALPHA * stencil(rho, z, col, centre)
        return 0

    lax.fori_loop(0, depth - 2 * REACH, sweep, 0)

    def last(z, _):
        centre = [field[z + REACH, col] for col in range(cols - 2 * REACH)]
        finish(
            z,
            [
                rho[z + HALO, col + HALO] + ALPHA * stencil(field, z, col, centre)
                for col in range(cols - 2 * HALO)
            ],
        )
        return 0

    lax.fori_loop(0, depth - 2 * HALO, last, 0)


def mixed(value, even, odd):
    rows = value.shape[0]
    return jnp.where(row_iota(rows) % 2 == 0, roll_rows(value, even), roll_rows(value, odd))


def same_body(swapped, final, *refs):
    if final:
        planes, acc_in, acc, partner, rho, field = refs
    else:
        flat, planes, acc, partner, rho, field = refs
        unpack(flat, planes)
    depth, cols, rows, _ = planes.shape

    def to_partner(value):
        return mixed(value, 1, 3) if swapped else roll_rows(value, 2)

    def from_partner(value):
        return mixed(value, -3, -1) if swapped else roll_rows(value, -2)

    def shift(z, _):
        for col in range(cols):
            partner[z, col] = to_partner(planes[z, col])
        return 0

    lax.fori_loop(0, depth, shift, 0)

    def finish(z, values):
        tiles = []
        for col, value in enumerate(values):
            own = value * partner[z + HALO, col + HALO]
            other = value * planes[z + HALO, col + HALO]
            total = own + from_partner(other)
            if final:
                tiles.append((total + acc_in[z, col]) * (-1.0 / CENTRE))
            else:
                acc[z, col] = total
        if final:
            repack(tiles, acc, z)

    potentials(planes, partner, rho, field, finish)


def cross_kernel(core_ref, planes, acc_in, flat, acc, travel, partner, rho, field, kept):
    depth, cols, rows, _ = planes.shape
    odd = core_ref[0] == 1
    unpack(flat, partner, lambda value: jnp.where(odd, value, roll_rows(value, 2)))

    def straight(z, values):
        for col, value in enumerate(values):
            acc[z, col] = acc_in[z, col] + value * partner[z + HALO, col + HALO]
            kept[z, col] = value * planes[z + HALO, col + HALO]

    potentials(planes, partner, rho, field, straight)

    def shift(z, _):
        for col in range(cols):
            partner[z, col] = mixed(partner[z, col], -1, 1)
        return 0

    lax.fori_loop(0, depth, shift, 0)

    def swapped(z, values):
        tiles = []
        for col, value in enumerate(values):
            acc[z, col] = acc[z, col] + value * partner[z + HALO, col + HALO]
            total = kept[z, col] + mixed(value * planes[z + HALO, col + HALO], -1, 1)
            total = jnp.where(odd, total, roll_rows(total, -2))
            tiles.append(total * (-1.0 / CENTRE))
        repack(tiles, travel, z)

    potentials(planes, partner, rho, field, swapped)


def split_body(*refs):
    mine, theirs, outs = refs[0], refs[1], refs[2:]
    depth, rows, span = mine.shape
    orbs = outs[0].shape[0]
    for z in range(0, depth, 8):
        top = min(z + 8, depth)
        for a in range(0, span, LANES):
            b = min(a + LANES, span)
            value = mine[z:top, :, a:b] + theirs[z:top, :, a:b]
            value = jnp.swapaxes(value, 0, 1)
            for slot, out in enumerate(outs):
                out[:, z:top, a:b] = value[slot * orbs : (slot + 1) * orbs]


def place_body(chips, chip_ref, *refs):
    ins, out = refs[:chips], refs[chips]
    chip = chip_ref[0]
    span = ins[0].shape[2]
    for behind in range(chips):
        for source in range(chips):

            @pl.when(lax.rem(chip + chips - behind, chips) == source)
            def _(behind=behind, source=source):
                out[:, :, source * span : (source + 1) * span] = ins[behind][...]


def per_device(n_band, orbitals):
    orbs, depth, total = orbitals.shape
    chips = n_band // 2
    width = total // NY // chips
    index = lax.axis_index("band")
    chip = (index // 2).astype(jnp.int32).reshape(1)
    core = (index % 2).astype(jnp.int32).reshape(1)

    def along(value, steps):
        pairs = [(i, (i + 2 * steps) % n_band) for i in range(n_band)]
        return lax.ppermute(value, "band", pairs)

    def partner_core(value):
        return lax.ppermute(value, "band", [(i, i ^ 1) for i in range(n_band)])

    n_slab = lax.axis_size("slab")
    up = [(i, (i + 1) % n_slab) for i in range(n_slab)]
    down = [(j, i) for i, j in up]
    below = lax.ppermute(orbitals[:, depth - HALO :], "slab", up)
    above = lax.ppermute(orbitals[:, :HALO], "slab", down)

    main = pack(chip, [orbitals], chips, width)
    main = [main[0]] + [along(main[s], s) for s in range(1, chips)]
    edge = pack(chip, [below, above], chips, width)
    edge = [edge[0]] + [along(edge[s], s) for s in range(1, chips)]
    order = [0] + list(range(chips - 1, 0, -1))
    flat = gather([main[s] for s in order], [edge[s] for s in order])
    other = partner_core(flat)

    rows = orbs * chips
    cols = width + 2 * HALO
    full = (depth + 2 * HALO, cols, rows, LANES)
    swept = (depth + 2 * REACH, cols - 2 * REACH, rows, LANES)
    inner = (depth, width, rows, LANES)
    scratch = [pltpu.VMEM(s, jnp.float32) for s in (full, full, swept)]
    points = rows * LANES * depth * cols
    planes, acc = call(
        functools.partial(same_body, False, False),
        [sds(*full), sds(*inner)],
        [flat],
        scratch=scratch,
        flops=40 * points,
        name="same",
    )
    acc, travel = call(
        cross_kernel,
        [sds(*inner), sds(depth, rows, width * NY)],
        [core, planes, acc, other],
        scratch=scratch + [pltpu.VMEM(inner, jnp.float32)],
        flops=80 * points,
        smem=True,
        name="cross",
    )
    back = partner_core(travel)
    mine = call(
        functools.partial(same_body, True, True),
        [sds(depth, rows, width * NY)],
        [planes, acc],
        scratch=scratch,
        flops=40 * points,
        name="same_swapped",
    )[0]
    parts = call(
        split_body,
        [sds(orbs, depth, width * NY)] * chips,
        [mine, back],
        name="split",
    )
    parts = [parts[0]] + [along(parts[s], s) for s in range(1, chips)]
    return call(
        functools.partial(place_body, chips),
        [sds(orbs, depth, total)],
        [chip, *parts],
        smem=True,
        name="place",
    )[0]


def solution(mesh):
    return jax.shard_map(
        functools.partial(per_device, mesh.shape["band"]),
        mesh=mesh,
        in_specs=(P("band", "slab", None),),
        out_specs=P("band", "slab", None),
        check_vma=False,
    )
```

```python
import functools

import jax
import jax.numpy as jnp
from jax import lax
from jax.experimental import pallas as pl
from jax.experimental.pallas import tpu as pltpu
from jax.sharding import PartitionSpec as P

NY = 72
LANES = 128
TILE = 256
WINDOW = 3 * TILE
REACH = 2
HALO = 4
CENTRE = 8.5
ALPHA = 1.0 / (12.0 * CENTRE)
VMEM = pl.BlockSpec(memory_space=pltpu.VMEM)
SMEM = pl.BlockSpec(memory_space=pltpu.SMEM)


def params(limit=None):
    return pltpu.CompilerParams(vmem_limit_bytes=limit)


def sds(*shape):
    return jax.ShapeDtypeStruct(shape, jnp.float32)


def call(body, out, inputs, scratch=(), flops=0, smem=False, limit=None, name=None):
    nbytes = sum(4 * x.size for x in inputs) + sum(4 * o.size for o in out)
    specs = [VMEM] * len(inputs)
    if smem:
        specs[0] = SMEM
    return pl.pallas_call(
        body,
        out_shape=out,
        in_specs=specs,
        out_specs=[VMEM] * len(out),
        scratch_shapes=scratch,
        compiler_params=params(limit),
        cost_estimate=pl.CostEstimate(flops=flops, bytes_accessed=nbytes, transcendentals=0),
        name=name,
    )(*inputs)


def pack_body(chips, width, n_in, *refs):
    chip_ref, ins, outs = refs[0], refs[1 : 1 + n_in], refs[1 + n_in :]
    chip = chip_ref[0]
    total = ins[0].shape[2]
    span = (width + 2 * HALO) * NY
    for ahead in range(chips):
        for target in range(chips):

            @pl.when(lax.rem(chip + ahead, chips) == target)
            def _(ahead=ahead, target=target):
                start = (target * width - HALO) * NY
                row = 0
                for ref in ins:
                    rows = ref.shape[1]
                    for orb in range(ref.shape[0]):
                        lo, hi = start, start + span
                        if lo < 0:
                            value = jnp.concatenate(
                                [ref[orb, :, lo + total : total], ref[orb, :, 0:hi]], axis=-1
                            )
                        elif hi > total:
                            value = jnp.concatenate(
                                [ref[orb, :, lo:total], ref[orb, :, 0 : hi - total]], axis=-1
                            )
                        else:
                            value = ref[orb, :, lo:hi]
                        outs[ahead][orb, row : row + rows, :] = value
                    row += rows


def pack(chip, pieces, chips, width):
    orbs = pieces[0].shape[0]
    rows = sum(p.shape[1] for p in pieces)
    span = (width + 2 * HALO) * NY
    return call(
        functools.partial(pack_body, chips, width, len(pieces)),
        [sds(orbs, rows, span)] * chips,
        [chip, *pieces],
        smem=True,
        name="pack",
    )


def gather_body(chips, *refs):
    main, edge, out = refs[:chips], refs[chips : 2 * chips], refs[2 * chips]
    orbs, depth, span = main[0].shape

    def move(sources, lo, hi, at):
        for a in range(0, span, LANES):
            b = min(a + LANES, span)
            value = jnp.concatenate([ref[:, lo:hi, a:b] for ref in sources], axis=0)
            out[at : at + hi - lo, :, a:b] = jnp.swapaxes(value, 0, 1)

    move(edge, 0, HALO, 0)
    for z in range(0, depth, 8):
        move(main, z, min(z + 8, depth), HALO + z)
    move(edge, HALO, 2 * HALO, HALO + depth)


def gather(main, edge):
    orbs, depth, span = main[0].shape
    chips = len(main)
    return call(
        functools.partial(gather_body, chips),
        [sds(depth + 2 * HALO, orbs * chips, span)],
        [*main, *edge],
        name="gather",
    )[0]


def row_mixed(value, even, odd):
    rows = value.shape[1]
    row = lax.broadcasted_iota(jnp.int32, value.shape, 1)
    return jnp.where(row % 2 == 0, roll_rows(value, even), roll_rows(value, odd))


def roll_rows(value, shift):
    return pltpu.roll(value, shift % value.shape[1], 1)


def n_tiles(span, sweeps):
    return -(-(span - sweeps * REACH * NY - LANES) // TILE)


def weights_body(out):
    i = lax.broadcasted_iota(jnp.int32, (WINDOW, TILE), 0)
    lane = lax.broadcasted_iota(jnp.int32, (1, TILE), 1)

    def tile(t, _):
        y = lax.rem(lane + (t * TILE + LANES), NY)
        at = lane + 2 * LANES
        near = (i == at - NY) | (i == at + NY)
        far = (i == at - 2 * NY) | (i == at + 2 * NY)
        for step in (1, -1):
            near |= i == at + step - jnp.where(y + step >= NY, NY, jnp.where(y + step < 0, -NY, 0))
        for step in (2, -2):
            far |= i == at + step - jnp.where(y + step >= NY, NY, jnp.where(y + step < 0, -NY, 0))
        value = jnp.where(near, 16.0, jnp.where(far, -1.0, 0.0))
        out[t] = value.astype(jnp.bfloat16)
        return 0

    lax.fori_loop(0, out.shape[0], tile, 0)


def weights(span):
    return pl.pallas_call(
        weights_body,
        out_shape=jax.ShapeDtypeStruct((n_tiles(span, 1), WINDOW, TILE), jnp.bfloat16),
        out_specs=VMEM,
        name="weights",
    )()


def halves(value):
    high = value.astype(jnp.bfloat16)
    return high, (value - high.astype(jnp.float32)).astype(jnp.bfloat16)


def in_plane(split_ref, first, rows, t, weight):
    lanes = pl.ds(pl.multiple_of(t * TILE, TILE), WINDOW)
    total = None
    for half in range(2):
        part = jnp.dot(
            split_ref[half, first : first + rows, lanes],
            weight,
            preferred_element_type=jnp.float32,
        )
        total = part if total is None else total + part
    return total


def off(split_ref, full_ref, n_rows, depth, t, weight):
    lanes = pl.ds(pl.multiple_of(t * TILE, TILE), TILE)

    def planes(z):
        return full_ref[z * n_rows : (z + depth) * n_rows, lanes]

    inside = in_plane(split_ref, REACH * n_rows, depth * n_rows, t, weight)
    near = planes(1) + planes(3)
    far = planes(0) + planes(4)
    return planes(2), inside + (16.0 * near - far)


def potentials(first, to_partner, second, w_ref, work, finish):
    rho_split, rho, mid_split, mid = work
    depth, n_rows, span = first.shape
    for ref in (rho_split, mid_split):
        edge = jnp.zeros((2, ref.shape[1], 2 * LANES), jnp.bfloat16)
        ref[:, :, 0 : 2 * LANES] = edge
    tail = (LANES + span) // LANES * LANES
    rho_split[:, :, tail:] = jnp.zeros(
        (2, rho_split.shape[1], rho_split.shape[2] - tail), jnp.bfloat16
    )
    held = rho.shape[1]
    tail = (span - LANES) // LANES * LANES
    if tail < held:
        rho[:, tail:] = jnp.zeros((rho.shape[0], held - tail), jnp.float32)
    step = 4

    def density(s, _):
        z = pl.multiple_of(s * step, step)
        rows = pl.ds(pl.multiple_of(s * (step * n_rows), step * n_rows), step * n_rows)
        for lo in range(0, span, LANES):
            hi = min(lo + LANES, span)
            value = first[pl.ds(z, step), :, lo:hi] * to_partner(second[pl.ds(z, step), :, lo:hi])
            value = value.reshape(step * n_rows, hi - lo)
            high, low = halves(value)
            rho_split[0, rows, lo + LANES : hi + LANES] = high
            rho_split[1, rows, lo + LANES : hi + LANES] = low
            if LANES <= lo < held + LANES:
                rho[rows, lo - LANES : hi - LANES] = value
        return 0

    lax.fori_loop(0, depth // step, density, 0)

    def sweep(t, _):
        centre, total = off(rho_split, rho, n_rows, depth - 2 * REACH, t, w_ref[t])
        value = centre + ALPHA * total
        high, low = halves(value)
        lanes = pl.ds(pl.multiple_of(t * TILE, TILE), TILE)
        mid[:, lanes] = value
        lanes = pl.ds(pl.multiple_of(t * TILE + 2 * LANES, LANES), TILE)
        mid_split[0, :, lanes] = high
        mid_split[1, :, lanes] = low
        return 0

    lax.fori_loop(0, w_ref.shape[0], sweep, 0)

    inner = depth - 2 * HALO

    def last(t, _):
        lanes = pl.ds(pl.multiple_of(t * TILE, TILE), TILE)
        _, total = off(mid_split, mid, n_rows, inner, t, w_ref[t])
        value = rho[HALO * n_rows : (HALO + inner) * n_rows, lanes] + ALPHA * total
        finish(lanes, pl.ds(pl.multiple_of(t * TILE + LANES, LANES), TILE), value.reshape(inner, n_rows, TILE))
        return 0

    lax.fori_loop(0, n_tiles(span, 2), last, 0)


def same_body(swapped, final, planes, w_ref, *refs):
    acc_in = refs[0] if final else None
    acc, *work = refs[1:] if final else refs
    inner = acc.shape[0]

    def to_partner(value):
        return row_mixed(value, 1, 3) if swapped else roll_rows(value, 2)

    def from_partner(value):
        return row_mixed(value, -3, -1) if swapped else roll_rows(value, -2)

    def finish(lanes, at, value):
        mine = planes[HALO : HALO + inner, :, at]
        total = value * to_partner(mine) + from_partner(value * mine)
        if final:
            total = (total + acc_in[:, :, lanes]) * (-1.0 / CENTRE)
        acc[:, :, lanes] = total

    potentials(planes, to_partner, planes, w_ref, work, finish)


def cross_body(core_ref, planes, w_ref, acc_in, flat, acc, travel, partner, *work):
    depth, n_rows, span = planes.shape
    inner = depth - 2 * HALO
    odd = core_ref[0] == 1

    def shift(z, _):
        for lo in range(0, span, LANES):
            hi = min(lo + LANES, span)
            value = flat[pl.ds(z * 4, 4), :, lo:hi]
            partner[pl.ds(z * 4, 4), :, lo:hi] = jnp.where(odd, value, roll_rows(value, 2))
        return 0

    lax.fori_loop(0, depth // 4, shift, 0)

    def straight(lanes, at, value):
        acc[:, :, lanes] = acc_in[:, :, lanes] + value * partner[HALO : HALO + inner, :, at]
        travel[:, :, lanes] = value * planes[HALO : HALO + inner, :, at]

    potentials(planes, lambda v: v, partner, w_ref, work, straight)

    def swap(value):
        return row_mixed(value, -1, 1)

    def swapped(lanes, at, value):
        acc[:, :, lanes] = acc[:, :, lanes] + value * swap(partner[HALO : HALO + inner, :, at])
        total = travel[:, :, lanes] + swap(value * planes[HALO : HALO + inner, :, at])
        travel[:, :, lanes] = jnp.where(odd, total, roll_rows(total, -2)) * (-1.0 / CENTRE)

    potentials(planes, swap, partner, w_ref, work, swapped)


def split_body(first, *refs):
    mine, theirs, outs = refs[0], refs[1], refs[2:]
    depth = mine.shape[0]
    orbs, _, span = outs[0].shape
    for z in range(0, depth, 8):
        top = min(z + 8, depth)
        for a in range(0, span, LANES):
            b = min(a + LANES, span)
            value = mine[z:top, :, first + a : first + b] + theirs[z:top, :, a:b]
            value = jnp.swapaxes(value, 0, 1)
            for slot, out in enumerate(outs):
                out[:, z:top, a:b] = value[slot * orbs : (slot + 1) * orbs]


def place_body(chips, first, chip_ref, *refs):
    ins, out = refs[:chips], refs[chips]
    chip = chip_ref[0]
    span = out.shape[2] // chips
    for behind in range(chips):
        for source in range(chips):

            @pl.when(lax.rem(chip + chips - behind, chips) == source)
            def _(behind=behind, source=source):
                out[:, :, source * span : (source + 1) * span] = ins[behind][
                    :, :, first : first + span
                ]


def per_device(n_band, orbitals):
    orbs, depth, total = orbitals.shape
    chips = n_band // 2
    width = total // NY // chips
    index = lax.axis_index("band")
    chip = (index // 2).astype(jnp.int32).reshape(1)
    core = (index % 2).astype(jnp.int32).reshape(1)

    def along(value, steps):
        pairs = [(i, (i + 2 * steps) % n_band) for i in range(n_band)]
        return lax.ppermute(value, "band", pairs)

    def partner_core(value):
        return lax.ppermute(value, "band", [(i, i ^ 1) for i in range(n_band)])

    n_slab = lax.axis_size("slab")
    up = [(i, (i + 1) % n_slab) for i in range(n_slab)]
    down = [(j, i) for i, j in up]
    below = lax.ppermute(orbitals[:, depth - HALO :], "slab", up)
    above = lax.ppermute(orbitals[:, :HALO], "slab", down)

    main = pack(chip, [orbitals], chips, width)
    main = [main[0]] + [along(main[s], s) for s in range(1, chips)]
    edge = pack(chip, [below, above], chips, width)
    edge = [edge[0]] + [along(edge[s], s) for s in range(1, chips)]
    order = [0] + list(range(chips - 1, 0, -1))
    flat = gather([main[s] for s in order], [edge[s] for s in order])
    other = partner_core(flat)

    rows = orbs * chips
    span = (width + 2 * HALO) * NY
    banded = weights(span)
    full = depth + 2 * HALO
    swept = depth + 2 * REACH
    tiles = n_tiles(span, 1)
    lanes = n_tiles(span, 2) * TILE
    work = [
        pltpu.VMEM((2, full * rows, tiles * TILE + WINDOW - TILE), jnp.bfloat16),
        pltpu.VMEM((full * rows, tiles * TILE), jnp.float32),
        pltpu.VMEM((2, swept * rows, tiles * TILE + WINDOW - TILE), jnp.bfloat16),
        pltpu.VMEM((swept * rows, tiles * TILE), jnp.float32),
    ]
    inner = sds(depth, rows, lanes)
    flops = 4 * WINDOW * TILE * tiles * full * rows * 2
    acc = call(
        functools.partial(same_body, False, False),
        [inner],
        [flat, banded],
        scratch=work,
        flops=flops,
        name="same",
    )[0]
    acc, travel = call(
        cross_body,
        [inner, inner],
        [core, flat, banded, acc, other],
        scratch=[pltpu.VMEM((full, rows, span), jnp.float32), *work],
        flops=2 * flops,
        smem=True,
        name="cross",
    )
    start = HALO * NY - LANES
    cut = start // LANES * LANES
    sent = start - cut + width * NY
    back = partner_core(travel[:, :, cut : cut + sent])
    mine = call(
        functools.partial(same_body, True, True),
        [inner],
        [flat, banded, acc],
        scratch=work,
        flops=flops,
        name="same_swapped",
    )[0]
    parts = call(
        functools.partial(split_body, cut),
        [sds(orbs, depth, sent)] * chips,
        [mine, back],
        name="split",
    )
    parts = [parts[0]] + [along(parts[s], s) for s in range(1, chips)]
    return call(
        functools.partial(place_body, chips, start - cut),
        [sds(orbs, depth, total)],
        [chip, *parts],
        smem=True,
        name="place",
    )[0]


def solution(mesh):
    return jax.shard_map(
        functools.partial(per_device, mesh.shape["band"]),
        mesh=mesh,
        in_specs=(P("band", "slab", None),),
        out_specs=P("band", "slab", None),
        check_vma=False,
    )
```

```python
import functools

import jax
import jax.numpy as jnp
from jax import lax
from jax.experimental import pallas as pl
from jax.experimental.pallas import tpu as pltpu
from jax.sharding import PartitionSpec as P


NY = 72
LANES = 128
TILE = 256
WINDOW = 3 * TILE
REACH = 2
HALO = 4
STEP = 4
CENTRE = 8.5
DIAGONAL = 12.0 * CENTRE
SCALE = -1.0 / (CENTRE * DIAGONAL * DIAGONAL)
VMEM = pl.BlockSpec(memory_space=pltpu.VMEM)
SMEM = pl.BlockSpec(memory_space=pltpu.SMEM)
ANY = pl.BlockSpec(memory_space=pl.ANY)


def sds(*shape):
    return jax.ShapeDtypeStruct(shape, jnp.float32)


def call(body, out, inputs, scratch=(), flops=0, smem=False, after=None, limit=12):
    nbytes = sum(4 * x.size for x in inputs) + sum(4 * o.size for o in out)
    specs = [VMEM] * len(inputs)
    if smem:
        specs[0] = SMEM
    if after is not None:
        inner = body
        inputs = [*inputs, after]
        specs.append(ANY)
        skip = len(inputs) - 1

        def body(*refs):
            inner(*refs[:skip], *refs[skip + 1 :])

    return pl.pallas_call(
        body,
        out_shape=out,
        in_specs=specs,
        out_specs=[VMEM] * len(out),
        scratch_shapes=scratch,
        compiler_params=pltpu.CompilerParams(vmem_limit_bytes=limit << 20),
        cost_estimate=pl.CostEstimate(flops=flops, bytes_accessed=nbytes, transcendentals=0),
    )(*inputs)


def floor_to(value, unit):
    return value // unit * unit


def ceil_to(value, unit):
    return -(-value // unit) * unit


class Ranges:
    def __init__(self, chips, total):
        self.chips = chips
        self.total = total
        self.width = total // chips
        self.halo = HALO * NY
        starts = [j * self.width - self.halo for j in range(chips)]
        self.starts = [floor_to(s, LANES) for s in starts]
        shifts = [s - a for s, a in zip(starts, self.starts)]
        low, high = min(shifts), max(shifts)
        used = self.width + 2 * self.halo
        self.length = ceil_to(high + used, LANES)
        reach = REACH * NY
        self.first = floor_to(low + reach, LANES)
        self.n_first = ceil_to(high + used - reach - self.first, TILE) // TILE
        self.second = floor_to(low + 2 * reach, LANES)
        self.n_second = ceil_to(high + used - 2 * reach - self.second, TILE) // TILE
        self.out_starts = [floor_to(j * self.width, LANES) for j in range(chips)]
        self.out_length = max(
            ceil_to((j + 1) * self.width, LANES) - s for j, s in enumerate(self.out_starts)
        )

    def shift(self, chip):
        start = chip * self.width - self.halo + ceil_to(self.halo, LANES)
        return lax.rem(start, LANES)

    def out_at(self, chip):
        start = chip * self.width
        return lax.div(start, LANES) * LANES - (start - self.halo - self.shift(chip)) - self.second

    @property
    def pad(self):
        return max(0, TILE - self.first)

    @property
    def split_length(self):
        ends = (
            self.pad + self.first - TILE + self.n_first * TILE + WINDOW - TILE,
            self.pad + self.second - TILE + self.n_second * TILE + WINDOW - TILE,
            self.pad + self.first + self.n_first * TILE,
            self.pad + self.length,
        )
        return ceil_to(max(ends), LANES)

    @property
    def full_length(self):
        return max(
            self.first + self.n_first * TILE, self.second + self.n_second * TILE, self.length
        )


def pack_body(ranges, chip_ref, *refs):
    chips, total, length = ranges.chips, ranges.total, ranges.length
    ins, outs = refs[:-chips], refs[-chips:]
    chip = chip_ref[0]
    for ahead in range(chips):
        for target in range(chips):

            @pl.when(lax.rem(chip + ahead, chips) == target)
            def _(ahead=ahead, start=ranges.starts[target]):
                row = 0
                for ref in ins:

                    def plane(z, _, ref=ref, row=row):
                        lo, hi = start, start + length
                        pieces = []
                        if lo < 0:
                            pieces.append(ref[z, :, lo + total : total])
                        pieces.append(ref[z, :, max(lo, 0) : min(hi, total)])
                        if hi > total:
                            pieces.append(ref[z, :, 0 : hi - total])
                        value = pieces[0] if len(pieces) == 1 else jnp.concatenate(pieces, axis=-1)
                        outs[ahead][row + z] = value
                        return 0

                    lax.fori_loop(0, ref.shape[0], plane, 0)
                    row += ref.shape[0]


def pack(ranges, chip, pieces):
    orbs = pieces[0].shape[1]
    rows = sum(p.shape[0] for p in pieces)
    return call(
        functools.partial(pack_body, ranges),
        [sds(rows, orbs, ranges.length)] * ranges.chips,
        [chip, *pieces],
        smem=True,
    )


def gather_body(*refs):
    ins, out = refs[:-1], refs[-1]
    orbs = ins[0].shape[1]

    def plane(z, _):
        for slot, ref in enumerate(ins):
            out[z, slot * orbs : (slot + 1) * orbs, :] = ref[z]
        return 0

    lax.fori_loop(0, out.shape[0], plane, 0)


def gather(pieces, after=None):
    depth, orbs, span = pieces[0].shape
    return call(gather_body, [sds(depth, orbs * len(pieces), span)], pieces, after=after)[0]


def roll_rows(value, shift):
    if isinstance(shift, int):
        shift = shift % value.shape[1]
        if shift == 0:
            return value
    return pltpu.roll(value, shift, 1)


class Pairing:
    def __init__(self, rows, even, odd=None):
        self.rows, self.even, self.odd = rows, even, odd

    def apply(self, value, even, odd):
        if odd is None:
            return roll_rows(value, even)
        row = lax.broadcasted_iota(jnp.int32, value.shape, 1)
        return jnp.where(row % 2 == 0, roll_rows(value, even), roll_rows(value, odd))

    def negative(self, shift):
        return -shift if isinstance(shift, int) else lax.rem(self.rows - shift, self.rows)

    def partner(self, value):
        return self.apply(value, self.even, self.odd)

    def back(self, value):
        if self.odd is None:
            return self.apply(value, self.negative(self.even), None)
        return self.apply(value, self.negative(self.odd), self.negative(self.even))


def weights_body(ranges, chip_ref, out):
    i = lax.broadcasted_iota(jnp.int32, (WINDOW, TILE), 0)
    lane = lax.broadcasted_iota(jnp.int32, (1, TILE), 1)
    shift = ranges.shift(chip_ref[0])
    at = lane + TILE

    def tile(t, start, diagonal):
        y = lax.rem(lane + (start + 2 * NY) - shift, NY)
        near = (i == at - NY) | (i == at + NY)
        far = (i == at - 2 * NY) | (i == at + 2 * NY)

        def beside(step):
            wrap = jnp.where(y + step >= NY, NY, jnp.where(y + step < 0, -NY, 0))
            return i == at + step - wrap

        near = near | beside(1) | beside(-1)
        far = far | beside(2) | beside(-2)
        value = jnp.where(i == at, diagonal, 0.0)
        value = jnp.where(near, 16.0, jnp.where(far, -1.0, value))
        out[t] = value.astype(jnp.bfloat16)

    def first(t, _):
        tile(t, ranges.first + t * TILE, DIAGONAL)
        return 0

    def second(t, _):
        tile(ranges.n_first + t, ranges.second + t * TILE, 0.0)
        return 0

    lax.fori_loop(0, ranges.n_first, first, 0)
    lax.fori_loop(0, ranges.n_second, second, 0)


def weights(ranges, chip):
    shape = (ranges.n_first + ranges.n_second, WINDOW, TILE)
    return pl.pallas_call(
        functools.partial(weights_body, ranges),
        out_shape=jax.ShapeDtypeStruct(shape, jnp.bfloat16),
        in_specs=[SMEM],
        out_specs=VMEM,
        name="weights",
    )(chip)


def store_halves(ref, rows, lanes, value):
    high = value.astype(jnp.bfloat16)
    ref[0, rows, lanes] = high
    ref[1, rows, lanes] = (value - high.astype(jnp.float32)).astype(jnp.bfloat16)


def aligned(start, size):
    if isinstance(start, int):
        return slice(start, start + size)
    return pl.ds(pl.multiple_of(start, LANES), size)


def tiles(count, product, use, buffer):
    def tile(t, _):
        product(t, buffer)
        use(t, buffer)
        return 0

    lax.fori_loop(0, count, tile, 0)


def potentials(ranges, first, second, pairing, w_ref, work, finish):
    rho_split, rho, mid_split, mid, product = work
    main, _ = first
    inner, n_rows, span = main.shape
    pad = ranges.pad

    def density(part, z, row):
        rows = pl.ds(row, STEP * n_rows)
        for lo in range(0, span, LANES):
            lanes = slice(lo, lo + LANES)
            value = first[part][pl.ds(z, STEP), :, lanes]
            value = value * pairing.partner(second[part][pl.ds(z, STEP), :, lanes])
            value = value.reshape(STEP * n_rows, LANES)
            store_halves(rho_split, rows, slice(lo + pad, lo + pad + LANES), value)
            rho[rows, lanes] = value

    density(1, 0, 0)

    def chunk(s, _):
        z = pl.multiple_of(s * STEP, STEP)
        density(0, z, pl.multiple_of(s * (STEP * n_rows) + HALO * n_rows, STEP * n_rows))
        return 0

    lax.fori_loop(0, inner // STEP, chunk, 0)
    density(1, HALO, (HALO + inner) * n_rows)

    def in_plane(source, planes, start, weight, out):
        lanes = aligned(start - TILE + pad, WINDOW)
        rows = planes * n_rows
        value = source[:, REACH * n_rows : REACH * n_rows + rows, lanes].reshape(2 * rows, WINDOW)
        out[0 : 2 * rows] = jnp.dot(value, weight, preferred_element_type=jnp.float32)

    def off(source, planes, start, inside):
        rows = planes * n_rows

        def shifted(z):
            return source[z * n_rows : z * n_rows + rows, aligned(start, TILE)]

        near = shifted(1) + shifted(3)
        far = shifted(0) + shifted(4)
        return (inside[0:rows] + inside[rows : 2 * rows]) + (16.0 * near - far)

    swept = inner + 2 * REACH

    def product_1(t, out):
        in_plane(rho_split, swept, ranges.first + t * TILE, w_ref[t], out)

    def use_1(t, inside):
        start = ranges.first + t * TILE
        value = off(rho, swept, start, inside)
        rows = slice(0, swept * n_rows)
        mid[rows, aligned(start, TILE)] = value
        store_halves(mid_split, rows, aligned(start + pad, TILE), value)

    tiles(ranges.n_first, product_1, use_1, product)

    def product_2(t, out):
        in_plane(mid_split, inner, ranges.second + t * TILE, w_ref[t + ranges.n_first], out)

    def use_2(t, inside):
        start = ranges.second + t * TILE
        here = aligned(start, TILE)
        value = off(mid, inner, start, inside)
        value = value + (DIAGONAL * DIAGONAL) * rho[HALO * n_rows : (HALO + inner) * n_rows, here]
        finish(here, aligned(t * TILE, TILE), value.reshape(inner, n_rows, TILE))

    tiles(ranges.n_second, product_2, use_2, product)


def clear(ranges, work):
    rho_split, rho, mid_split, mid = work[:4]
    span = ranges.length

    def zero(ref, lo, hi):
        if lo < hi:
            shape = ref.shape[:-1] + (hi - lo,)
            ref[..., lo:hi] = jnp.zeros(shape, ref.dtype)

    pad, end = ranges.pad, ranges.split_length
    zero(rho_split, 0, pad)
    zero(rho_split, pad + span, end)
    zero(rho, span, rho.shape[-1])
    zero(mid_split, 0, pad + ranges.first)
    zero(mid_split, pad + ranges.first + ranges.n_first * TILE, end)
    zero(mid, 0, ranges.first)
    zero(mid, ranges.first + ranges.n_first * TILE, mid.shape[-1])


def same_body(ranges, swapped, final, main, edge, w_ref, *refs):
    acc_in = refs[0] if final else None
    acc, *work = refs[1:] if final else refs
    n_rows = main.shape[1]
    pairing = Pairing(n_rows, 1, 3) if swapped else Pairing(n_rows, 2)

    def finish(here, lanes, value):
        mine = main[:, :, here]
        total = value * pairing.partner(mine) + pairing.back(value * mine)
        if final:
            total = (total + acc_in[:, :, lanes]) * SCALE
        acc[:, :, lanes] = total

    clear(ranges, work)
    planes = (main, edge)
    potentials(ranges, planes, planes, pairing, w_ref, work, finish)


def cross_body(ranges, core_ref, main, edge, w_ref, acc_in, other, other_edge, acc, travel, *work):
    n_rows = main.shape[1]
    odd = core_ref[0] == 1
    straight = Pairing(n_rows, jnp.where(odd, 0, 2))
    swapped = Pairing(n_rows, jnp.where(odd, n_rows - 1, 1), jnp.where(odd, 1, 3))

    def finish_straight(here, lanes, value):
        acc[:, :, lanes] = acc_in[:, :, lanes] + value * straight.partner(other[:, :, here])
        travel[:, :, lanes] = straight.back(value * main[:, :, here])

    def finish_swapped(here, lanes, value):
        acc[:, :, lanes] = acc[:, :, lanes] + value * swapped.partner(other[:, :, here])
        total = travel[:, :, lanes] + swapped.back(value * main[:, :, here])
        travel[:, :, lanes] = total * SCALE

    clear(ranges, work)
    planes, others = (main, edge), (other, other_edge)
    potentials(ranges, planes, others, straight, w_ref, work, finish_straight)
    potentials(ranges, planes, others, swapped, w_ref, work, finish_swapped)


def split_body(ranges, chip_ref, mine, theirs, *outs):
    orbs = outs[0].shape[1]
    lanes = aligned(ranges.out_at(chip_ref[0]), ranges.out_length)

    def plane(z, _):
        value = mine[z, :, lanes] + theirs[z, :, lanes]
        for slot, out in enumerate(outs):
            out[z] = value[slot * orbs : (slot + 1) * orbs]
        return 0

    lax.fori_loop(0, outs[0].shape[0], plane, 0)


def place_body(ranges, chip_ref, *refs):
    chips = ranges.chips
    ins, out = refs[:chips], refs[chips]
    chip = chip_ref[0]
    for behind in range(chips):
        for source in range(chips):

            @pl.when(lax.rem(chip + chips - behind, chips) == source)
            def _(ref=ins[behind], source=source):
                base = ranges.out_starts[source]
                lo, hi = source * ranges.width, (source + 1) * ranges.width

                def plane(z, _):
                    at = lo
                    while at < hi:
                        stop = min(floor_to(at, LANES) + LANES, hi)
                        if at % LANES == 0:
                            whole = max(floor_to(hi, LANES), stop)
                            stop = whole
                        out[z, :, at:stop] = ref[z, :, at - base : stop - base]
                        at = stop
                    return 0

                lax.fori_loop(0, out.shape[0], plane, 0)


def per_device(n_band, orbitals):
    orbs, depth, total = orbitals.shape
    chips = n_band // 2
    ranges = Ranges(chips, total)
    index = lax.axis_index("band")
    chip = (index // 2).astype(jnp.int32).reshape(1)
    core = (index % 2).astype(jnp.int32).reshape(1)
    planes = jnp.transpose(orbitals, (1, 0, 2))

    def along(value, steps):
        pairs = [(i, (i + 2 * steps) % n_band) for i in range(n_band)]
        return lax.ppermute(value, "band", pairs)

    def partner_core(value):
        return lax.ppermute(value, "band", [(i, i ^ 1) for i in range(n_band)])

    n_slab = lax.axis_size("slab")
    up = [(i, (i + 1) % n_slab) for i in range(n_slab)]
    down = [(j, i) for i, j in up]
    below = lax.ppermute(planes[depth - HALO :], "slab", up)
    above = lax.ppermute(planes[:HALO], "slab", down)

    order = [0] + list(range(chips - 1, 0, -1))

    def spread(pieces):
        sent = pack(ranges, chip, pieces)
        got = [sent[0]]
        for s in range(1, chips):
            got.append(along(sent[s], s))
        return [got[s] for s in order]

    banded = weights(ranges, chip)
    main = gather(spread([planes]), after=banded)
    edge = gather(spread([below, above]))
    other, other_edge = partner_core(main), partner_core(edge)

    rows = orbs * chips
    full, swept = (depth + 2 * HALO) * rows, (depth + 2 * REACH) * rows
    work = [
        pltpu.VMEM((2, full, ranges.split_length), jnp.bfloat16),
        pltpu.VMEM((full, ranges.full_length), jnp.float32),
        pltpu.VMEM((2, swept, ranges.split_length), jnp.bfloat16),
        pltpu.VMEM((swept, ranges.full_length), jnp.float32),
        pltpu.VMEM((2 * swept, TILE), jnp.float32),
    ]
    inner = sds(depth, rows, ranges.n_second * TILE)
    flops = 4 * WINDOW * TILE * (ranges.n_first + ranges.n_second) * full
    acc = call(
        functools.partial(same_body, ranges, False, False),
        [inner],
        [main, edge, banded],
        scratch=work,
        flops=flops,
        limit=40,
    )[0]
    acc, travel = call(
        functools.partial(cross_body, ranges),
        [inner, inner],
        [core, main, edge, banded, acc, other, other_edge],
        scratch=work,
        flops=2 * flops,
        smem=True,
        limit=40,
    )
    back = partner_core(travel)
    mine = call(
        functools.partial(same_body, ranges, True, True),
        [inner],
        [main, edge, banded, acc],
        scratch=work,
        flops=flops,
        limit=40,
    )[0]
    parts = call(
        functools.partial(split_body, ranges),
        [sds(depth, orbs, ranges.out_length)] * chips,
        [chip, mine, back],
        smem=True,
    )
    parts = [parts[0]] + [along(parts[s], s) for s in range(1, chips)]
    result = call(
        functools.partial(place_body, ranges), [sds(depth, orbs, total)], [chip, *parts], smem=True
    )[0]
    return jnp.transpose(result, (1, 0, 2))


def solution(mesh):
    def body(orbitals):
        return per_device(mesh.shape["band"], orbitals)

    return jax.shard_map(
        body,
        mesh=mesh,
        in_specs=(P("band", "slab", None),),
        out_specs=P("band", "slab", None),
        check_vma=False,
    )
```

```python
import functools

import jax
import jax.numpy as jnp
from jax import lax
from jax.experimental import pallas as pl
from jax.experimental.pallas import tpu as pltpu
from jax.sharding import PartitionSpec as P


NY = 72
LANES = 128
TILE = 256
WINDOW = 3 * TILE
REACH = 2
HALO = 4
KERNEL_MIB = 36
CHUNKS = 2
STEP = 2
CENTRE = 8.5
DIAGONAL = 12.0 * CENTRE
SCALE = -1.0 / (CENTRE * DIAGONAL * DIAGONAL)
VMEM = pl.BlockSpec(memory_space=pltpu.VMEM)
SMEM = pl.BlockSpec(memory_space=pltpu.SMEM)


def sds(*shape):
    return jax.ShapeDtypeStruct(shape, jnp.float32)


def call(body, out, inputs, scratch=(), flops=0, smem=False, limit=12):
    nbytes = sum(4 * x.size for x in inputs) + sum(4 * o.size for o in out)
    specs = [VMEM] * len(inputs)
    if smem:
        specs[0] = SMEM
    return pl.pallas_call(
        body,
        out_shape=out,
        in_specs=specs,
        out_specs=[VMEM] * len(out),
        scratch_shapes=scratch,
        compiler_params=pltpu.CompilerParams(vmem_limit_bytes=limit << 20),
        cost_estimate=pl.CostEstimate(flops=flops, bytes_accessed=nbytes, transcendentals=0),
    )(*inputs)


def floor_to(value, unit):
    return value // unit * unit


def ceil_to(value, unit):
    return -(-value // unit) * unit


class Ranges:
    def __init__(self, chips, total):
        self.chips = chips
        self.total = total
        self.width = total // chips
        self.halo = HALO * NY
        starts = [j * self.width - self.halo for j in range(chips)]
        self.starts = [floor_to(s, LANES) for s in starts]
        shifts = [s - a for s, a in zip(starts, self.starts)]
        low, high = min(shifts), max(shifts)
        used = self.width + 2 * self.halo
        self.length = ceil_to(high + used, LANES)
        reach = REACH * NY
        self.first = floor_to(low + reach, LANES)
        self.n_first = ceil_to(high + used - reach - self.first, TILE) // TILE
        self.second = floor_to(low + 2 * reach, LANES)
        self.n_second = ceil_to(high + used - 2 * reach - self.second, TILE) // TILE
        self.out_starts = [floor_to(j * self.width, LANES) for j in range(chips)]
        self.out_length = max(
            ceil_to((j + 1) * self.width, LANES) - s for j, s in enumerate(self.out_starts)
        )

    def shift(self, chip):
        start = chip * self.width - self.halo + ceil_to(self.halo, LANES)
        return lax.rem(start, LANES)

    def out_at(self, chip):
        start = chip * self.width
        return lax.div(start, LANES) * LANES - (start - self.halo - self.shift(chip)) - self.second

    @property
    def pad(self):
        return max(0, TILE - self.first)

    @property
    def split_length(self):
        ends = (
            self.pad + self.first - TILE + self.n_first * TILE + WINDOW - TILE,
            self.pad + self.second - TILE + self.n_second * TILE + WINDOW - TILE,
            self.pad + self.first + self.n_first * TILE,
            self.pad + self.length,
        )
        return ceil_to(max(ends), LANES)

    @property
    def full_length(self):
        return max(
            self.first + self.n_first * TILE, self.second + self.n_second * TILE, self.length
        )


def pack_body(ranges, bounds, chip_ref, *refs):
    chips, total, length = ranges.chips, ranges.total, ranges.length
    ins, outs = refs[:-chips], refs[-chips:]
    chip = chip_ref[0]
    for ahead in range(chips):
        for target in range(chips):

            @pl.when(lax.rem(chip + ahead, chips) == target)
            def _(ahead=ahead, start=ranges.starts[target]):
                row = 0
                for ref, (low, high) in zip(ins, bounds):

                    def plane(s, _, ref=ref, row=row - low, low=low):
                        z = low + s * STEP
                        lo, hi = start, start + length
                        at = pl.ds(z, STEP)
                        pieces = []
                        if lo < 0:
                            pieces.append(ref[at, :, lo + total : total])
                        pieces.append(ref[at, :, max(lo, 0) : min(hi, total)])
                        if hi > total:
                            pieces.append(ref[at, :, 0 : hi - total])
                        value = pieces[0] if len(pieces) == 1 else jnp.concatenate(pieces, axis=-1)
                        outs[ahead][pl.ds(row + z, STEP)] = value
                        return 0

                    lax.fori_loop(0, (high - low) // STEP, plane, 0)
                    row += high - low


def pack(ranges, chip, pieces):
    orbs = pieces[0][0].shape[1]
    bounds = [(low, high) for _, low, high in pieces]
    rows = sum(high - low for low, high in bounds)
    return call(
        functools.partial(pack_body, ranges, bounds),
        [sds(rows, orbs, ranges.length)] * ranges.chips,
        [chip, *(array for array, _, _ in pieces)],
        smem=True,
    )


def gather_body(groups, kept, *refs):
    out = refs[-1]
    row = 0
    if kept:
        before = refs[0]
        out[0:kept] = before[before.shape[0] - kept :]
        refs, row = refs[1:], kept
    slots = (len(refs) - 1) // groups
    for group in range(groups):
        ins = refs[group * slots : (group + 1) * slots]
        orbs = ins[0].shape[1]

        def plane(s, _, ins=ins, row=row):
            z = s * STEP
            for slot, ref in enumerate(ins):
                value = ref[pl.ds(z, STEP)]
                out[pl.ds(row + z, STEP), slot * orbs : (slot + 1) * orbs, :] = value
            return 0

        lax.fori_loop(0, ins[0].shape[0] // STEP, plane, 0)
        row += ins[0].shape[0]


def gather(groups, before=None, kept=0):
    depth = kept + sum(g[0].shape[0] for g in groups)
    _, orbs, span = groups[0][0].shape
    return call(
        functools.partial(gather_body, len(groups), kept),
        [sds(depth, orbs * len(groups[0]), span)],
        [*([before] if kept else []), *(p for g in groups for p in g)],
    )[0]


def roll_rows(value, shift):
    if isinstance(shift, int):
        shift = shift % value.shape[1]
        if shift == 0:
            return value
    return pltpu.roll(value, shift, 1)


class Pairing:
    def __init__(self, rows, even, odd=None):
        self.rows, self.even, self.odd = rows, even, odd

    def apply(self, value, even, odd):
        if odd is None:
            return roll_rows(value, even)
        row = lax.broadcasted_iota(jnp.int32, value.shape, 1)
        return jnp.where(row % 2 == 0, roll_rows(value, even), roll_rows(value, odd))

    def negative(self, shift):
        return -shift if isinstance(shift, int) else lax.rem(self.rows - shift, self.rows)

    def partner(self, value):
        return self.apply(value, self.even, self.odd)

    def back(self, value):
        if self.odd is None:
            return self.apply(value, self.negative(self.even), None)
        return self.apply(value, self.negative(self.odd), self.negative(self.even))


def weights_body(ranges, chip_ref, out):
    i = lax.broadcasted_iota(jnp.int32, (WINDOW, TILE), 0)
    lane = lax.broadcasted_iota(jnp.int32, (1, TILE), 1)
    shift = ranges.shift(chip_ref[0])
    at = lane + TILE

    def tile(t, start, diagonal):
        y = lax.rem(lane + (start + 2 * NY) - shift, NY)
        near = (i == at - NY) | (i == at + NY)
        far = (i == at - 2 * NY) | (i == at + 2 * NY)

        def beside(step):
            wrap = jnp.where(y + step >= NY, NY, jnp.where(y + step < 0, -NY, 0))
            return i == at + step - wrap

        near = near | beside(1) | beside(-1)
        far = far | beside(2) | beside(-2)
        value = jnp.where(i == at, diagonal, 0.0)
        value = jnp.where(near, 16.0, jnp.where(far, -1.0, value))
        out[t] = value.astype(jnp.bfloat16)

    def first(t, _):
        tile(t, ranges.first + t * TILE, DIAGONAL)
        return 0

    def second(t, _):
        tile(ranges.n_first + t, ranges.second + t * TILE, 0.0)
        return 0

    lax.fori_loop(0, ranges.n_first, first, 0)
    lax.fori_loop(0, ranges.n_second, second, 0)


def weights(ranges, chip):
    shape = (ranges.n_first + ranges.n_second, WINDOW, TILE)
    out = jax.ShapeDtypeStruct(shape, jnp.bfloat16)
    return call(functools.partial(weights_body, ranges), [out], [chip], smem=True)[0]


def store_halves(ref, rows, lanes, value):
    high = value.astype(jnp.bfloat16)
    ref[0, rows, lanes] = high
    ref[1, rows, lanes] = (value - high.astype(jnp.float32)).astype(jnp.bfloat16)


def aligned(start, size):
    if isinstance(start, int):
        return slice(start, start + size)
    return pl.ds(pl.multiple_of(start, LANES), size)


def potentials(ranges, first, seconds, pairings, w_ref, work, finish):
    rho_split, rho, mid_split, mid, product = work
    depth, n_rows, span = first.shape
    inner = depth - 2 * HALO
    swept = inner + 2 * REACH
    pad = ranges.pad
    kinds = len(seconds)

    def density(s, _):
        planes = pl.ds(s * STEP, STEP)
        rows = pl.ds(pl.multiple_of(s * (STEP * n_rows), STEP * n_rows), STEP * n_rows)
        for lo in range(0, span, LANES):
            lanes = slice(lo, lo + LANES)
            mine = first[planes, :, lanes]
            for k, (second, pairing) in enumerate(zip(seconds, pairings)):
                value = mine * pairing.partner(second[planes, :, lanes])
                value = value.reshape(STEP * n_rows, LANES)
                store_halves(rho_split.at[k], rows, slice(lo + pad, lo + pad + LANES), value)
                rho[k, rows, lanes] = value
        return 0

    lax.fori_loop(0, depth // STEP, density, 0)

    def in_plane(source, planes, start, weight):
        lanes = aligned(start - TILE + pad, WINDOW)
        rows = planes * n_rows
        value = source[:, :, REACH * n_rows : REACH * n_rows + rows, lanes]
        value = value.reshape(2 * kinds * rows, WINDOW)
        product[0 : 2 * kinds * rows] = jnp.dot(value, weight, preferred_element_type=jnp.float32)

    def off(source, k, planes, start):
        rows = planes * n_rows

        def shifted(z):
            return source[k, z * n_rows : z * n_rows + rows, aligned(start, TILE)]

        near = shifted(1) + shifted(3)
        far = shifted(0) + shifted(4)
        row = 2 * k * rows
        inside = product[row : row + rows] + product[row + rows : row + 2 * rows]
        return inside + (16.0 * near - far)

    def sweep(t, _):
        start = ranges.first + t * TILE
        in_plane(rho_split, swept, start, w_ref[t])
        for k in range(kinds):
            value = off(rho, k, swept, start)
            mid[k, :, aligned(start, TILE)] = value
            store_halves(mid_split.at[k], slice(None), aligned(start + pad, TILE), value)
        return 0

    lax.fori_loop(0, ranges.n_first, sweep, 0)

    def last(t, _):
        start = ranges.second + t * TILE
        here = aligned(start, TILE)
        in_plane(mid_split, inner, start, w_ref[t + ranges.n_first])
        values = []
        for k in range(kinds):
            value = off(mid, k, inner, start)
            source = rho[k, HALO * n_rows : (HALO + inner) * n_rows, here]
            value = value + (DIAGONAL * DIAGONAL) * source
            values.append(value.reshape(inner, n_rows, TILE))
        finish(here, aligned(t * TILE, TILE), values)
        return 0

    lax.fori_loop(0, ranges.n_second, last, 0)


def clear(ranges, work):
    rho_split, rho, mid_split, mid = work[:4]
    span = ranges.length

    def zero(ref, lo, hi):
        if lo < hi:
            shape = ref.shape[:-1] + (hi - lo,)
            ref[..., lo:hi] = jnp.zeros(shape, ref.dtype)

    pad, end = ranges.pad, ranges.split_length
    zero(rho_split, 0, pad)
    zero(rho_split, pad + span, end)
    zero(rho, span, rho.shape[-1])
    zero(mid_split, 0, pad + ranges.first)
    zero(mid_split, pad + ranges.first + ranges.n_first * TILE, end)
    zero(mid, 0, ranges.first)
    zero(mid, ranges.first + ranges.n_first * TILE, mid.shape[-1])


def total_of(acc_in, lanes, total):
    return total if acc_in is None else (total + acc_in[:, :, lanes]) * SCALE


def same_body(ranges, follows, planes, w_ref, *refs):
    acc_in = refs[0] if follows else None
    acc, *work = refs[1:] if follows else refs
    depth, n_rows, _ = planes.shape
    inner = slice(HALO, depth - HALO)
    pairings = (Pairing(n_rows, 2), Pairing(n_rows, 1, 3))

    def finish(here, lanes, values):
        mine = planes[inner, :, here]
        total = None
        for value, pairing in zip(values, pairings):
            part = value * pairing.partner(mine) + pairing.back(value * mine)
            total = part if total is None else total + part
        acc[:, :, lanes] = total_of(acc_in, lanes, total)

    clear(ranges, work)
    potentials(ranges, planes, (planes, planes), pairings, w_ref, work, finish)


def cross_body(ranges, follows, core_ref, planes, w_ref, other, *refs):
    acc_in = refs[0] if follows else None
    acc, travel, *work = refs[1:] if follows else refs
    depth, n_rows, _ = planes.shape
    inner = slice(HALO, depth - HALO)
    odd = core_ref[0] == 1
    pairings = (
        Pairing(n_rows, jnp.where(odd, 0, 2)),
        Pairing(n_rows, jnp.where(odd, n_rows - 1, 1), jnp.where(odd, 1, 3)),
    )

    def finish(here, lanes, values):
        mine, theirs = planes[inner, :, here], other[inner, :, here]
        own = away = None
        for value, pairing in zip(values, pairings):
            to_own = value * pairing.partner(theirs)
            to_away = pairing.back(value * mine)
            own = to_own if own is None else own + to_own
            away = to_away if away is None else away + to_away
        acc[:, :, lanes] = total_of(acc_in, lanes, own)
        travel[:, :, lanes] = away * SCALE

    clear(ranges, work)
    potentials(ranges, planes, (other, other), pairings, w_ref, work, finish)


def split_body(ranges, chip_ref, mine, theirs, *outs):
    orbs = outs[0].shape[1]
    lanes = aligned(ranges.out_at(chip_ref[0]), ranges.out_length)

    def plane(s, _):
        at = pl.ds(s * STEP, STEP)
        value = mine[at, :, lanes] + theirs[at, :, lanes]
        for slot, out in enumerate(outs):
            out[at] = value[:, slot * orbs : (slot + 1) * orbs]
        return 0

    lax.fori_loop(0, outs[0].shape[0] // STEP, plane, 0)


def place_body(ranges, chip_ref, *refs):
    chips = ranges.chips
    ins, out = refs[:-1], refs[-1]
    chip = chip_ref[0]
    for behind in range(chips):
        for source in range(chips):

            @pl.when(lax.rem(chip + chips - behind, chips) == source)
            def _(parts=ins[behind::chips], source=source):
                base = ranges.out_starts[source]
                lo, hi = source * ranges.width, (source + 1) * ranges.width
                row = 0
                for ref in parts:

                    def plane(s, _, ref=ref, row=row):
                        at = pl.ds(s * STEP, STEP)
                        into = pl.ds(row + s * STEP, STEP)
                        lane = lo
                        while lane < hi:
                            stop = min(floor_to(lane, LANES) + LANES, hi)
                            if lane % LANES == 0:
                                stop = max(floor_to(hi, LANES), stop)
                            out[into, :, lane:stop] = ref[at, :, lane - base : stop - base]
                            lane = stop
                        return 0

                    lax.fori_loop(0, ref.shape[0] // STEP, plane, 0)
                    row += ref.shape[0]


def per_device(n_band, orbitals):
    orbs, depth, total = orbitals.shape
    chips = n_band // 2
    ranges = Ranges(chips, total)
    index = lax.axis_index("band")
    chip = (index // 2).astype(jnp.int32).reshape(1)
    core = (index % 2).astype(jnp.int32).reshape(1)
    planes = jnp.transpose(orbitals, (1, 0, 2))

    def along(value, steps):
        pairs = [(i, (i + 2 * steps) % n_band) for i in range(n_band)]
        return lax.ppermute(value, "band", pairs)

    def partner_core(value):
        return lax.ppermute(value, "band", [(i, i ^ 1) for i in range(n_band)])

    n_slab = lax.axis_size("slab")
    up = [(i, (i + 1) % n_slab) for i in range(n_slab)]
    down = [(j, i) for i, j in up]
    below = lax.ppermute(planes[depth - HALO :], "slab", up)
    above = lax.ppermute(planes[:HALO], "slab", down)

    order = [0] + list(range(chips - 1, 0, -1))

    def spread(sent):
        got = [sent[0]]
        for s in range(1, chips):
            got.append(along(sent[s], s))
        return got

    def fetch(pieces):
        sent = pack(ranges, chip, pieces)
        got = spread(sent)
        return [got[s] for s in order]

    inner = depth // CHUNKS
    cut = inner + HALO
    got_a = fetch([(planes, 0, cut)])
    banded = weights(ranges, chip)
    got_low = fetch([(below, 0, HALO)])
    got_b = fetch([(planes, cut, depth), (above, 0, HALO)])
    planes_a = gather([got_low, got_a])
    planes_b = gather([got_b], before=planes_a, kept=2 * HALO)

    rows = orbs * chips
    full, swept = (inner + 2 * HALO) * rows, (inner + 2 * REACH) * rows
    work = [
        pltpu.VMEM((2, 2, full, ranges.split_length), jnp.bfloat16),
        pltpu.VMEM((2, full, ranges.full_length), jnp.float32),
        pltpu.VMEM((2, 2, swept, ranges.split_length), jnp.bfloat16),
        pltpu.VMEM((2, swept, ranges.full_length), jnp.float32),
        pltpu.VMEM((4 * swept, TILE), jnp.float32),
    ]
    result = sds(inner, rows, ranges.n_second * TILE)
    flops = 8 * WINDOW * TILE * (ranges.n_first + ranges.n_second) * full

    def same(mine, *acc):
        return call(
            functools.partial(same_body, ranges, bool(acc)),
            [result],
            [mine, banded, *acc],
            scratch=work,
            flops=flops,
            limit=KERNEL_MIB,
        )[0]

    def cross(mine, other, *acc):
        own, travel = call(
            functools.partial(cross_body, ranges, bool(acc)),
            [result, result],
            [core, mine, banded, other, *acc],
            scratch=work,
            flops=flops,
            smem=True,
            limit=KERNEL_MIB,
        )
        return own, partner_core(travel)

    def give(acc, back):
        parts = call(
            functools.partial(split_body, ranges),
            [sds(inner, orbs, ranges.out_length)] * chips,
            [chip, acc, back],
            smem=True,
        )
        return spread(parts)

    other_a = partner_core(planes_a)
    acc_a = same(planes_a)
    other_b = partner_core(planes_b)
    acc_a, back_a = cross(planes_a, other_a, acc_a)
    acc_b, back_b = cross(planes_b, other_b)
    home = give(acc_a, back_a)
    acc_b = same(planes_b, acc_b)
    home += give(acc_b, back_b)
    out = call(
        functools.partial(place_body, ranges), [sds(depth, orbs, total)], [chip, *home], smem=True
    )[0]
    return jnp.transpose(out, (1, 0, 2))


def solution(mesh):
    def body(orbitals):
        return per_device(mesh.shape["band"], orbitals)

    return jax.shard_map(
        body,
        mesh=mesh,
        in_specs=(P("band", "slab", None),),
        out_specs=P("band", "slab", None),
        check_vma=False,
    )
```

```python
import functools

import jax
import jax.numpy as jnp
from jax import lax
from jax.experimental import pallas as pl
from jax.experimental.pallas import tpu as pltpu
from jax.sharding import PartitionSpec as P


NY = 72
LANES = 128
TILE = 256
WINDOW = 3 * TILE
REACH = 2
HALO = 4
CHUNKS = 2
STEP = 2
CENTRE = 8.5
DIAGONAL = 12.0 * CENTRE
SCALE = -1.0 / (CENTRE * DIAGONAL * DIAGONAL)
VMEM = pl.BlockSpec(memory_space=pltpu.VMEM)
SMEM = pl.BlockSpec(memory_space=pltpu.SMEM)


def sds(*shape):
    return jax.ShapeDtypeStruct(shape, jnp.float32)


def call(body, out, inputs, scratch=(), flops=0, smem=False, limit=12):
    nbytes = sum(4 * x.size for x in inputs) + sum(4 * o.size for o in out)
    specs = [VMEM] * len(inputs)
    if smem:
        specs[0] = SMEM
    return pl.pallas_call(
        body,
        out_shape=out,
        in_specs=specs,
        out_specs=[VMEM] * len(out),
        scratch_shapes=scratch,
        compiler_params=pltpu.CompilerParams(vmem_limit_bytes=limit << 20),
        cost_estimate=pl.CostEstimate(flops=flops, bytes_accessed=nbytes, transcendentals=0),
    )(*inputs)


def floor_to(value, unit):
    return value // unit * unit


def ceil_to(value, unit):
    return -(-value // unit) * unit


class Ranges:
    def __init__(self, chips, total):
        self.chips = chips
        self.total = total
        self.width = total // chips
        self.halo = HALO * NY
        starts = [j * self.width - self.halo for j in range(chips)]
        self.starts = [floor_to(s, LANES) for s in starts]
        shifts = [s - a for s, a in zip(starts, self.starts)]
        low, high = min(shifts), max(shifts)
        used = self.width + 2 * self.halo
        self.length = ceil_to(high + used, LANES)
        reach = REACH * NY
        self.first = floor_to(low + reach, LANES)
        self.n_first = ceil_to(high + used - reach - self.first, TILE) // TILE
        self.second = floor_to(low + 2 * reach, LANES)
        self.n_second = ceil_to(high + used - 2 * reach - self.second, TILE) // TILE
        self.out_starts = [floor_to(j * self.width, LANES) for j in range(chips)]
        self.out_length = max(
            ceil_to((j + 1) * self.width, LANES) - s for j, s in enumerate(self.out_starts)
        )

    def shift(self, chip):
        start = chip * self.width - self.halo + ceil_to(self.halo, LANES)
        return lax.rem(start, LANES)

    def out_at(self, chip):
        start = chip * self.width
        return lax.div(start, LANES) * LANES - (start - self.halo - self.shift(chip)) - self.second

    @property
    def pad(self):
        return max(0, TILE - self.first)

    @property
    def split_length(self):
        ends = (
            self.pad + self.first - TILE + self.n_first * TILE + WINDOW - TILE,
            self.pad + self.second - TILE + self.n_second * TILE + WINDOW - TILE,
            self.pad + self.first + self.n_first * TILE,
            self.pad + self.length,
        )
        return ceil_to(max(ends), LANES)

    @property
    def full_length(self):
        return max(
            self.first + self.n_first * TILE, self.second + self.n_second * TILE, self.length
        )


def pack_body(ranges, bounds, chip_ref, *refs):
    chips, total, length = ranges.chips, ranges.total, ranges.length
    ins, outs = refs[:-chips], refs[-chips:]
    chip = chip_ref[0]
    for ahead in range(chips):
        for target in range(chips):

            @pl.when(lax.rem(chip + ahead, chips) == target)
            def _(ahead=ahead, start=ranges.starts[target]):
                row = 0
                for ref, (low, high) in zip(ins, bounds):

                    def plane(s, _, ref=ref, row=row - low, low=low):
                        z = low + s * STEP
                        lo, hi = start, start + length
                        at = pl.ds(z, STEP)
                        pieces = []
                        if lo < 0:
                            pieces.append(ref[at, :, lo + total : total])
                        pieces.append(ref[at, :, max(lo, 0) : min(hi, total)])
                        if hi > total:
                            pieces.append(ref[at, :, 0 : hi - total])
                        value = pieces[0] if len(pieces) == 1 else jnp.concatenate(pieces, axis=-1)
                        outs[ahead][pl.ds(row + z, STEP)] = value
                        return 0

                    lax.fori_loop(0, (high - low) // STEP, plane, 0)
                    row += high - low


def pack(ranges, chip, pieces):
    orbs = pieces[0][0].shape[1]
    bounds = [(low, high) for _, low, high in pieces]
    rows = sum(high - low for low, high in bounds)
    return call(
        functools.partial(pack_body, ranges, bounds),
        [sds(rows, orbs, ranges.length)] * ranges.chips,
        [chip, *(array for array, _, _ in pieces)],
        smem=True,
    )


def gather_body(groups, kept, unread, *refs):
    refs, out = refs[unread:], refs[-1]
    row = 0
    if kept:
        before = refs[0]
        out[0:kept] = before[before.shape[0] - kept :]
        refs, row = refs[1:], kept
    slots = (len(refs) - 1) // groups
    for group in range(groups):
        ins = refs[group * slots : (group + 1) * slots]
        orbs = ins[0].shape[1]

        def plane(s, _, ins=ins, row=row):
            z = s * STEP
            for slot, ref in enumerate(ins):
                value = ref[pl.ds(z, STEP)]
                out[pl.ds(row + z, STEP), slot * orbs : (slot + 1) * orbs, :] = value
            return 0

        lax.fori_loop(0, ins[0].shape[0] // STEP, plane, 0)
        row += ins[0].shape[0]


def gather(groups, before=None, kept=0, alive=()):
    depth = kept + sum(g[0].shape[0] for g in groups)
    _, orbs, span = groups[0][0].shape
    return call(
        functools.partial(gather_body, len(groups), kept, len(alive)),
        [sds(depth, orbs * len(groups[0]), span)],
        [*alive, *([before] if kept else []), *(p for g in groups for p in g)],
    )[0]


def roll_rows(value, shift):
    if isinstance(shift, int):
        shift = shift % value.shape[1]
        if shift == 0:
            return value
    return pltpu.roll(value, shift, 1)


class Pairing:
    def __init__(self, rows, even, odd=None):
        self.rows, self.even, self.odd = rows, even, odd

    def apply(self, value, even, odd):
        if odd is None:
            return roll_rows(value, even)
        row = lax.broadcasted_iota(jnp.int32, value.shape, 1)
        return jnp.where(row % 2 == 0, roll_rows(value, even), roll_rows(value, odd))

    def negative(self, shift):
        return -shift if isinstance(shift, int) else lax.rem(self.rows - shift, self.rows)

    def partner(self, value):
        return self.apply(value, self.even, self.odd)

    def back(self, value):
        if self.odd is None:
            return self.apply(value, self.negative(self.even), None)
        return self.apply(value, self.negative(self.odd), self.negative(self.even))


def weights_body(ranges, chip_ref, out):
    i = lax.broadcasted_iota(jnp.int32, (WINDOW, TILE), 0)
    lane = lax.broadcasted_iota(jnp.int32, (1, TILE), 1)
    shift = ranges.shift(chip_ref[0])
    at = lane + TILE

    def tile(t, start, diagonal):
        y = lax.rem(lane + (start + 2 * NY) - shift, NY)
        near = (i == at - NY) | (i == at + NY)
        far = (i == at - 2 * NY) | (i == at + 2 * NY)

        def beside(step):
            wrap = jnp.where(y + step >= NY, NY, jnp.where(y + step < 0, -NY, 0))
            return i == at + step - wrap

        near = near | beside(1) | beside(-1)
        far = far | beside(2) | beside(-2)
        value = jnp.where(i == at, diagonal, 0.0)
        value = jnp.where(near, 16.0, jnp.where(far, -1.0, value))
        out[t] = value.astype(jnp.bfloat16)

    def first(t, _):
        tile(t, ranges.first + t * TILE, DIAGONAL)
        return 0

    def second(t, _):
        tile(ranges.n_first + t, ranges.second + t * TILE, 0.0)
        return 0

    lax.fori_loop(0, ranges.n_first, first, 0)
    lax.fori_loop(0, ranges.n_second, second, 0)


def weights(ranges, chip):
    shape = (ranges.n_first + ranges.n_second, WINDOW, TILE)
    out = jax.ShapeDtypeStruct(shape, jnp.bfloat16)
    return call(functools.partial(weights_body, ranges), [out], [chip], smem=True)[0]


def store_halves(ref, rows, lanes, value):
    high = value.astype(jnp.bfloat16)
    ref[0, rows, lanes] = high
    ref[1, rows, lanes] = (value - high.astype(jnp.float32)).astype(jnp.bfloat16)


def aligned(start, size):
    if isinstance(start, int):
        return slice(start, start + size)
    return pl.ds(pl.multiple_of(start, LANES), size)


def potentials(ranges, first, seconds, pairings, w_ref, work, finish):
    rho_split, rho, mid_split, mid, product = work
    depth, n_rows, span = first.shape
    inner = depth - 2 * HALO
    swept = inner + 2 * REACH
    pad = ranges.pad
    kinds = len(seconds)

    def density(s, _):
        planes = pl.ds(s * STEP, STEP)
        rows = pl.ds(pl.multiple_of(s * (STEP * n_rows), STEP * n_rows), STEP * n_rows)
        for lo in range(0, span, LANES):
            lanes = slice(lo, lo + LANES)
            mine = first[planes, :, lanes]
            for k, (second, pairing) in enumerate(zip(seconds, pairings)):
                value = mine * pairing.partner(second[planes, :, lanes])
                value = value.reshape(STEP * n_rows, LANES)
                store_halves(rho_split.at[k], rows, slice(lo + pad, lo + pad + LANES), value)
                rho[k, rows, lanes] = value
        return 0

    lax.fori_loop(0, depth // STEP, density, 0)

    def in_plane(source, planes, start, weight):
        lanes = aligned(start - TILE + pad, WINDOW)
        rows = planes * n_rows
        value = source[:, :, REACH * n_rows : REACH * n_rows + rows, lanes]
        value = value.reshape(2 * kinds * rows, WINDOW)
        product[0 : 2 * kinds * rows] = jnp.dot(value, weight, preferred_element_type=jnp.float32)

    def off(source, k, planes, start):
        rows = planes * n_rows

        def shifted(z):
            return source[k, z * n_rows : z * n_rows + rows, aligned(start, TILE)]

        near = shifted(1) + shifted(3)
        far = shifted(0) + shifted(4)
        row = 2 * k * rows
        inside = product[row : row + rows] + product[row + rows : row + 2 * rows]
        return inside + (16.0 * near - far)

    def sweep(t, _):
        start = ranges.first + t * TILE
        in_plane(rho_split, swept, start, w_ref[t])
        for k in range(kinds):
            value = off(rho, k, swept, start)
            mid[k, :, aligned(start, TILE)] = value
            store_halves(mid_split.at[k], slice(None), aligned(start + pad, TILE), value)
        return 0

    lax.fori_loop(0, ranges.n_first, sweep, 0)

    def last(t, _):
        start = ranges.second + t * TILE
        here = aligned(start, TILE)
        in_plane(mid_split, inner, start, w_ref[t + ranges.n_first])
        values = []
        for k in range(kinds):
            value = off(mid, k, inner, start)
            source = rho[k, HALO * n_rows : (HALO + inner) * n_rows, here]
            value = value + (DIAGONAL * DIAGONAL) * source
            values.append(value.reshape(inner, n_rows, TILE))
        finish(here, aligned(t * TILE, TILE), values)
        return 0

    lax.fori_loop(0, ranges.n_second, last, 0)


def clear(ranges, work):
    rho_split, rho, mid_split, mid = work[:4]
    span = ranges.length

    def zero(ref, lo, hi):
        if lo < hi:
            shape = ref.shape[:-1] + (hi - lo,)
            ref[..., lo:hi] = jnp.zeros(shape, ref.dtype)

    pad, end = ranges.pad, ranges.split_length
    zero(rho_split, 0, pad)
    zero(rho_split, pad + span, end)
    zero(rho, span, rho.shape[-1])
    zero(mid_split, 0, pad + ranges.first)
    zero(mid_split, pad + ranges.first + ranges.n_first * TILE, end)
    zero(mid, 0, ranges.first)
    zero(mid, ranges.first + ranges.n_first * TILE, mid.shape[-1])


def total_of(acc_in, lanes, total):
    return total if acc_in is None else (total + acc_in[:, :, lanes]) * SCALE


def same_body(ranges, follows, planes, w_ref, *refs):
    acc_in = refs[0] if follows else None
    acc, *work = refs[1:] if follows else refs
    depth, n_rows, _ = planes.shape
    inner = slice(HALO, depth - HALO)
    pairings = (Pairing(n_rows, 2), Pairing(n_rows, 1, 3))

    def finish(here, lanes, values):
        mine = planes[inner, :, here]
        total = None
        for value, pairing in zip(values, pairings):
            part = value * pairing.partner(mine) + pairing.back(value * mine)
            total = part if total is None else total + part
        acc[:, :, lanes] = total_of(acc_in, lanes, total)

    clear(ranges, work)
    potentials(ranges, planes, (planes, planes), pairings, w_ref, work, finish)


def cross_body(ranges, follows, chip_ref, planes, w_ref, other, *refs):
    acc_in = refs[0] if follows else None
    acc, travel, *work = refs[1:] if follows else refs
    depth, n_rows, _ = planes.shape
    inner = slice(HALO, depth - HALO)
    odd = chip_ref[1] == 1
    pairings = (
        Pairing(n_rows, jnp.where(odd, 0, 2)),
        Pairing(n_rows, jnp.where(odd, n_rows - 1, 1), jnp.where(odd, 1, 3)),
    )

    def finish(here, lanes, values):
        mine, theirs = planes[inner, :, here], other[inner, :, here]
        own = away = None
        for value, pairing in zip(values, pairings):
            to_own = value * pairing.partner(theirs)
            to_away = pairing.back(value * mine)
            own = to_own if own is None else own + to_own
            away = to_away if away is None else away + to_away
        acc[:, :, lanes] = total_of(acc_in, lanes, own)
        travel[:, :, lanes] = away * SCALE

    clear(ranges, work)
    potentials(ranges, planes, (other, other), pairings, w_ref, work, finish)


def split_body(ranges, chip_ref, mine, theirs, *outs):
    orbs = outs[0].shape[1]
    lanes = aligned(ranges.out_at(chip_ref[0]), ranges.out_length)

    def plane(s, _):
        at = pl.ds(s * STEP, STEP)
        value = mine[at, :, lanes] + theirs[at, :, lanes]
        for slot, out in enumerate(outs):
            out[at] = value[:, slot * orbs : (slot + 1) * orbs]
        return 0

    lax.fori_loop(0, outs[0].shape[0] // STEP, plane, 0)


def place_body(ranges, chip_ref, *refs):
    chips = ranges.chips
    ins, out = refs[:-1], refs[-1]
    chip = chip_ref[0]
    for behind in range(chips):
        for source in range(chips):

            @pl.when(lax.rem(chip + chips - behind, chips) == source)
            def _(parts=ins[behind::chips], source=source):
                base = ranges.out_starts[source]
                lo, hi = source * ranges.width, (source + 1) * ranges.width
                row = 0
                for ref in parts:

                    def plane(s, _, ref=ref, row=row):
                        at = pl.ds(s * STEP, STEP)
                        into = pl.ds(row + s * STEP, STEP)
                        lane = lo
                        while lane < hi:
                            stop = min(floor_to(lane, LANES) + LANES, hi)
                            if lane % LANES == 0:
                                stop = max(floor_to(hi, LANES), stop)
                            out[into, :, lane:stop] = ref[at, :, lane - base : stop - base]
                            lane = stop
                        return 0

                    lax.fori_loop(0, ref.shape[0] // STEP, plane, 0)
                    row += ref.shape[0]


def per_device(n_band, orbitals):
    orbs, depth, total = orbitals.shape
    chips = n_band // 2
    ranges = Ranges(chips, total)
    index = lax.axis_index("band")
    chip = jnp.stack([index // 2, index % 2]).astype(jnp.int32)
    planes = jnp.transpose(orbitals, (1, 0, 2))

    def along(value, steps):
        pairs = [(i, (i + 2 * steps) % n_band) for i in range(n_band)]
        return lax.ppermute(value, "band", pairs)

    def partner_core(value):
        return lax.ppermute(value, "band", [(i, i ^ 1) for i in range(n_band)])

    n_slab = lax.axis_size("slab")
    up = [(i, (i + 1) % n_slab) for i in range(n_slab)]
    down = [(j, i) for i, j in up]
    below = lax.ppermute(planes[depth - HALO :], "slab", up)
    above = lax.ppermute(planes[:HALO], "slab", down)

    order = [0] + list(range(chips - 1, 0, -1))

    def spread(sent):
        got = [sent[0]]
        for s in range(1, chips):
            got.append(along(sent[s], s))
        return got

    def fetch(pieces):
        sent = pack(ranges, chip, pieces)
        got = spread(sent)
        return [got[s] for s in order]

    inner = depth // CHUNKS
    cut = inner + HALO
    got_a = fetch([(planes, 0, cut)])
    banded = weights(ranges, chip)
    got_low = fetch([(below, 0, HALO)])
    got_b = fetch([(planes, cut, depth), (above, 0, HALO)])
    planes_a = gather([got_low, got_a])

    rows = orbs * chips
    full, swept = (inner + 2 * HALO) * rows, (inner + 2 * REACH) * rows
    work = [
        pltpu.VMEM((2, 2, full, ranges.split_length), jnp.bfloat16),
        pltpu.VMEM((2, full, ranges.full_length), jnp.float32),
        pltpu.VMEM((2, 2, swept, ranges.split_length), jnp.bfloat16),
        pltpu.VMEM((2, swept, ranges.full_length), jnp.float32),
        pltpu.VMEM((4 * swept, TILE), jnp.float32),
    ]
    result = sds(inner, rows, ranges.n_second * TILE)
    flops = 8 * WINDOW * TILE * (ranges.n_first + ranges.n_second) * full

    def same(mine, *acc):
        return call(
            functools.partial(same_body, ranges, bool(acc)),
            [result],
            [mine, banded, *acc],
            scratch=work,
            flops=flops,
            limit=12 + 12 * (rows // 8),
        )[0]

    def cross(mine, other, *acc):
        own, travel = call(
            functools.partial(cross_body, ranges, bool(acc)),
            [result, result],
            [chip, mine, banded, other, *acc],
            scratch=work,
            flops=flops,
            smem=True,
            limit=12 + 12 * (rows // 8),
        )
        return own, partner_core(travel)

    def give(acc, back):
        parts = call(
            functools.partial(split_body, ranges),
            [sds(inner, orbs, ranges.out_length)] * chips,
            [chip, acc, back],
            smem=True,
        )
        return spread(parts)

    other_a = partner_core(planes_a)
    acc_a = same(planes_a)
    planes_b = gather([got_b], before=planes_a, kept=2 * HALO, alive=(banded, acc_a))
    other_b = partner_core(planes_b)
    acc_a, back_a = cross(planes_a, other_a, acc_a)
    acc_b, back_b = cross(planes_b, other_b)
    home = give(acc_a, back_a)
    acc_b = same(planes_b, acc_b)
    home += give(acc_b, back_b)
    out = call(
        functools.partial(place_body, ranges), [sds(depth, orbs, total)], [chip, *home], smem=True
    )[0]
    return jnp.transpose(out, (1, 0, 2))


def solution(mesh):
    def body(orbitals):
        return per_device(mesh.shape["band"], orbitals)

    return jax.shard_map(
        body,
        mesh=mesh,
        in_specs=(P("band", "slab", None),),
        out_specs=P("band", "slab", None),
        check_vma=False,
    )
```

```python
import functools

import jax
import jax.numpy as jnp
from jax import lax
from jax.experimental import pallas as pl
from jax.experimental.pallas import tpu as pltpu
from jax.sharding import PartitionSpec as P


NY = 72
LANES = 128
TILE = 256
WINDOW = 3 * TILE
REACH = 2
HALO = 4
CHUNKS = 2
STEP = 2
CENTRE = 8.5
DIAGONAL = 12.0 * CENTRE
SCALE = -1.0 / (CENTRE * DIAGONAL * DIAGONAL)
VMEM = pl.BlockSpec(memory_space=pltpu.VMEM)
SMEM = pl.BlockSpec(memory_space=pltpu.SMEM)


def sds(*shape):
    return jax.ShapeDtypeStruct(shape, jnp.float32)


def call(body, out, inputs, scratch=(), flops=0, smem=False, limit=12):
    nbytes = sum(4 * x.size for x in inputs) + sum(4 * o.size for o in out)
    specs = [VMEM] * len(inputs)
    if smem:
        specs[0] = SMEM
    return pl.pallas_call(
        body,
        out_shape=out,
        in_specs=specs,
        out_specs=[VMEM] * len(out),
        scratch_shapes=scratch,
        compiler_params=pltpu.CompilerParams(vmem_limit_bytes=limit << 20),
        cost_estimate=pl.CostEstimate(flops=flops, bytes_accessed=nbytes, transcendentals=0),
    )(*inputs)


def floor_to(value, unit):
    return value // unit * unit


def ceil_to(value, unit):
    return -(-value // unit) * unit


class Ranges:
    def __init__(self, chips, total):
        self.chips = chips
        self.total = total
        self.width = total // chips
        self.halo = HALO * NY
        starts = [j * self.width - self.halo for j in range(chips)]
        self.starts = [floor_to(s, LANES) for s in starts]
        shifts = [s - a for s, a in zip(starts, self.starts)]
        low, high = min(shifts), max(shifts)
        used = self.width + 2 * self.halo
        self.length = ceil_to(high + used, LANES)
        reach = REACH * NY
        self.first = floor_to(low + reach, LANES)
        self.n_first = ceil_to(high + used - reach - self.first, TILE) // TILE
        self.second = floor_to(low + 2 * reach, LANES)
        self.n_second = ceil_to(high + used - 2 * reach - self.second, TILE) // TILE
        self.out_starts = [floor_to(j * self.width, LANES) for j in range(chips)]
        self.out_length = max(
            ceil_to((j + 1) * self.width, LANES) - s for j, s in enumerate(self.out_starts)
        )

    def shift(self, chip):
        start = chip * self.width - self.halo + ceil_to(self.halo, LANES)
        return lax.rem(start, LANES)

    def out_at(self, chip):
        start = chip * self.width
        return lax.div(start, LANES) * LANES - (start - self.halo - self.shift(chip)) - self.second

    @property
    def pad(self):
        return max(0, TILE - self.first)

    @property
    def split_length(self):
        ends = (
            self.pad + self.first - TILE + self.n_first * TILE + WINDOW - TILE,
            self.pad + self.second - TILE + self.n_second * TILE + WINDOW - TILE,
            self.pad + self.first + self.n_first * TILE,
            self.pad + self.length,
        )
        return ceil_to(max(ends), LANES)

    @property
    def full_length(self):
        return max(
            self.first + self.n_first * TILE, self.second + self.n_second * TILE, self.length
        )


def pack_body(ranges, bounds, chip_ref, *refs):
    chips, total, length = ranges.chips, ranges.total, ranges.length
    ins, outs = refs[:-chips], refs[-chips:]
    chip = chip_ref[0]
    for ahead in range(chips):
        for target in range(chips):

            @pl.when(lax.rem(chip + ahead, chips) == target)
            def _(ahead=ahead, start=ranges.starts[target]):
                row = 0
                for ref, (low, high) in zip(ins, bounds):

                    def plane(s, _, ref=ref, row=row - low, low=low):
                        z = low + s * STEP
                        lo, hi = start, start + length
                        at = pl.ds(z, STEP)
                        pieces = []
                        if lo < 0:
                            pieces.append(ref[at, :, lo + total : total])
                        pieces.append(ref[at, :, max(lo, 0) : min(hi, total)])
                        if hi > total:
                            pieces.append(ref[at, :, 0 : hi - total])
                        value = pieces[0] if len(pieces) == 1 else jnp.concatenate(pieces, axis=-1)
                        outs[ahead][pl.ds(row + z, STEP)] = value
                        return 0

                    lax.fori_loop(0, (high - low) // STEP, plane, 0)
                    row += high - low


def pack(ranges, chip, pieces):
    orbs = pieces[0][0].shape[1]
    bounds = [(low, high) for _, low, high in pieces]
    rows = sum(high - low for low, high in bounds)
    return call(
        functools.partial(pack_body, ranges, bounds),
        [sds(rows, orbs, ranges.length)] * ranges.chips,
        [chip, *(array for array, _, _ in pieces)],
        smem=True,
    )


def gather_body(groups, kept, unread, *refs):
    refs, out = refs[unread:], refs[-1]
    row = 0
    if kept:
        before = refs[0]
        out[0:kept] = before[before.shape[0] - kept :]
        refs, row = refs[1:], kept
    slots = (len(refs) - 1) // groups
    for group in range(groups):
        ins = refs[group * slots : (group + 1) * slots]
        orbs = ins[0].shape[1]

        def plane(s, _, ins=ins, row=row):
            z = s * STEP
            for slot, ref in enumerate(ins):
                value = ref[pl.ds(z, STEP)]
                out[pl.ds(row + z, STEP), slot * orbs : (slot + 1) * orbs, :] = value
            return 0

        lax.fori_loop(0, ins[0].shape[0] // STEP, plane, 0)
        row += ins[0].shape[0]


def gather(groups, before=None, kept=0, alive=()):
    depth = kept + sum(g[0].shape[0] for g in groups)
    _, orbs, span = groups[0][0].shape
    return call(
        functools.partial(gather_body, len(groups), kept, len(alive)),
        [sds(depth, orbs * len(groups[0]), span)],
        [*alive, *([before] if kept else []), *(p for g in groups for p in g)],
    )[0]


def roll_rows(value, shift):
    if isinstance(shift, int):
        shift = shift % value.shape[1]
        if shift == 0:
            return value
    return pltpu.roll(value, shift, 1)


class Pairing:
    def __init__(self, rows, even, odd=None):
        self.rows, self.even, self.odd = rows, even, odd

    def apply(self, value, even, odd):
        if odd is None:
            return roll_rows(value, even)
        row = lax.broadcasted_iota(jnp.int32, value.shape, 1)
        return jnp.where(row % 2 == 0, roll_rows(value, even), roll_rows(value, odd))

    def negative(self, shift):
        return -shift if isinstance(shift, int) else lax.rem(self.rows - shift, self.rows)

    def partner(self, value):
        return self.apply(value, self.even, self.odd)

    def back(self, value):
        if self.odd is None:
            return self.apply(value, self.negative(self.even), None)
        return self.apply(value, self.negative(self.odd), self.negative(self.even))


def weights_body(ranges, chip_ref, out):
    i = lax.broadcasted_iota(jnp.int32, (WINDOW, TILE), 0)
    lane = lax.broadcasted_iota(jnp.int32, (1, TILE), 1)
    shift = ranges.shift(chip_ref[0])
    at = lane + TILE

    def tile(t, start, diagonal):
        y = lax.rem(lane + (start + 2 * NY) - shift, NY)
        near = (i == at - NY) | (i == at + NY)
        far = (i == at - 2 * NY) | (i == at + 2 * NY)

        def beside(step):
            wrap = jnp.where(y + step >= NY, NY, jnp.where(y + step < 0, -NY, 0))
            return i == at + step - wrap

        near = near | beside(1) | beside(-1)
        far = far | beside(2) | beside(-2)
        value = jnp.where(i == at, diagonal, 0.0)
        value = jnp.where(near, 16.0, jnp.where(far, -1.0, value))
        out[t] = value.astype(jnp.bfloat16)

    def first(t, _):
        tile(t, ranges.first + t * TILE, DIAGONAL)
        return 0

    def second(t, _):
        tile(ranges.n_first + t, ranges.second + t * TILE, 0.0)
        return 0

    lax.fori_loop(0, ranges.n_first, first, 0)
    lax.fori_loop(0, ranges.n_second, second, 0)


def weights(ranges, chip):
    shape = (ranges.n_first + ranges.n_second, WINDOW, TILE)
    out = jax.ShapeDtypeStruct(shape, jnp.bfloat16)
    return call(functools.partial(weights_body, ranges), [out], [chip], smem=True)[0]


def store_halves(ref, rows, lanes, value):
    high = value.astype(jnp.bfloat16)
    ref[0, rows, lanes] = high
    ref[1, rows, lanes] = (value - high.astype(jnp.float32)).astype(jnp.bfloat16)


def aligned(start, size):
    if isinstance(start, int):
        return slice(start, start + size)
    return pl.ds(pl.multiple_of(start, LANES), size)


def potentials(ranges, first, seconds, pairings, w_ref, work, finish):
    rho_split, rho, mid_split, mid, *products = work
    depth, n_rows, span = first.shape
    inner = depth - 2 * HALO
    swept = inner + 2 * REACH
    pad = ranges.pad
    kinds = len(seconds)

    def density(s, _):
        planes = pl.ds(s * STEP, STEP)
        rows = pl.ds(pl.multiple_of(s * (STEP * n_rows), STEP * n_rows), STEP * n_rows)
        for lo in range(0, span, LANES):
            lanes = slice(lo, lo + LANES)
            mine = first[planes, :, lanes]
            for k, (second, pairing) in enumerate(zip(seconds, pairings)):
                value = mine * pairing.partner(second[planes, :, lanes])
                value = value.reshape(STEP * n_rows, LANES)
                store_halves(rho_split.at[k], rows, slice(lo + pad, lo + pad + LANES), value)
                rho[k, rows, lanes] = value
        return 0

    lax.fori_loop(0, depth // STEP, density, 0)

    def in_plane(source, planes, start, weight, product):
        lanes = aligned(start - TILE + pad, WINDOW)
        rows = planes * n_rows
        value = source[:, :, REACH * n_rows : REACH * n_rows + rows, lanes]
        value = value.reshape(2 * kinds * rows, WINDOW)
        product[0 : 2 * kinds * rows] = jnp.dot(value, weight, preferred_element_type=jnp.float32)

    def off(source, k, planes, start, product):
        rows = planes * n_rows

        def shifted(z):
            return source[k, z * n_rows : z * n_rows + rows, aligned(start, TILE)]

        near = shifted(1) + shifted(3)
        far = shifted(0) + shifted(4)
        row = 2 * k * rows
        inside = product[row : row + rows] + product[row + rows : row + 2 * rows]
        return inside + (16.0 * near - far)

    def pipelined(count, multiply, use):
        multiply(0, products[0])
        for t in range(count):
            if t + 1 < count:
                multiply(t + 1, products[(t + 1) % 2])
            use(t, products[t % 2])

    def multiply_1(t, product):
        in_plane(rho_split, swept, ranges.first + t * TILE, w_ref[t], product)

    def use_1(t, product):
        start = ranges.first + t * TILE
        for k in range(kinds):
            value = off(rho, k, swept, start, product)
            mid[k, :, aligned(start, TILE)] = value
            store_halves(mid_split.at[k], slice(None), aligned(start + pad, TILE), value)

    pipelined(ranges.n_first, multiply_1, use_1)

    def multiply_2(t, product):
        start = ranges.second + t * TILE
        in_plane(mid_split, inner, start, w_ref[t + ranges.n_first], product)

    def use_2(t, product):
        start = ranges.second + t * TILE
        here = aligned(start, TILE)
        values = []
        for k in range(kinds):
            value = off(mid, k, inner, start, product)
            source = rho[k, HALO * n_rows : (HALO + inner) * n_rows, here]
            value = value + (DIAGONAL * DIAGONAL) * source
            values.append(value.reshape(inner, n_rows, TILE))
        finish(here, aligned(t * TILE, TILE), values)

    pipelined(ranges.n_second, multiply_2, use_2)


def clear(ranges, work):
    rho_split, rho, mid_split, mid = work[:4]
    span = ranges.length

    def zero(ref, lo, hi):
        if lo < hi:
            shape = ref.shape[:-1] + (hi - lo,)
            ref[..., lo:hi] = jnp.zeros(shape, ref.dtype)

    pad, end = ranges.pad, ranges.split_length
    zero(rho_split, 0, pad)
    zero(rho_split, pad + span, end)
    zero(rho, span, rho.shape[-1])
    zero(mid_split, 0, pad + ranges.first)
    zero(mid_split, pad + ranges.first + ranges.n_first * TILE, end)
    zero(mid, 0, ranges.first)
    zero(mid, ranges.first + ranges.n_first * TILE, mid.shape[-1])


def total_of(acc_in, lanes, total):
    return total if acc_in is None else (total + acc_in[:, :, lanes]) * SCALE


def same_body(ranges, follows, planes, w_ref, *refs):
    acc_in = refs[0] if follows else None
    acc, *work = refs[1:] if follows else refs
    depth, n_rows, _ = planes.shape
    inner = slice(HALO, depth - HALO)
    pairings = (Pairing(n_rows, 2), Pairing(n_rows, 1, 3))

    def finish(here, lanes, values):
        mine = planes[inner, :, here]
        total = None
        for value, pairing in zip(values, pairings):
            part = value * pairing.partner(mine) + pairing.back(value * mine)
            total = part if total is None else total + part
        acc[:, :, lanes] = total_of(acc_in, lanes, total)

    clear(ranges, work)
    potentials(ranges, planes, (planes, planes), pairings, w_ref, work, finish)


def cross_body(ranges, follows, chip_ref, planes, w_ref, other, *refs):
    acc_in = refs[0] if follows else None
    acc, travel, *work = refs[1:] if follows else refs
    depth, n_rows, _ = planes.shape
    inner = slice(HALO, depth - HALO)
    odd = chip_ref[1] == 1
    pairings = (
        Pairing(n_rows, jnp.where(odd, 0, 2)),
        Pairing(n_rows, jnp.where(odd, n_rows - 1, 1), jnp.where(odd, 1, 3)),
    )

    def finish(here, lanes, values):
        mine, theirs = planes[inner, :, here], other[inner, :, here]
        own = away = None
        for value, pairing in zip(values, pairings):
            to_own = value * pairing.partner(theirs)
            to_away = pairing.back(value * mine)
            own = to_own if own is None else own + to_own
            away = to_away if away is None else away + to_away
        acc[:, :, lanes] = total_of(acc_in, lanes, own)
        travel[:, :, lanes] = away * SCALE

    clear(ranges, work)
    potentials(ranges, planes, (other, other), pairings, w_ref, work, finish)


def split_body(ranges, chip_ref, mine, theirs, *outs):
    orbs = outs[0].shape[1]
    lanes = aligned(ranges.out_at(chip_ref[0]), ranges.out_length)

    def plane(s, _):
        at = pl.ds(s * STEP, STEP)
        value = mine[at, :, lanes] + theirs[at, :, lanes]
        for slot, out in enumerate(outs):
            out[at] = value[:, slot * orbs : (slot + 1) * orbs]
        return 0

    lax.fori_loop(0, outs[0].shape[0] // STEP, plane, 0)


def place_body(ranges, chip_ref, *refs):
    chips = ranges.chips
    ins, out = refs[:-1], refs[-1]
    chip = chip_ref[0]
    for behind in range(chips):
        for source in range(chips):

            @pl.when(lax.rem(chip + chips - behind, chips) == source)
            def _(parts=ins[behind::chips], source=source):
                base = ranges.out_starts[source]
                lo, hi = source * ranges.width, (source + 1) * ranges.width
                row = 0
                for ref in parts:

                    def plane(s, _, ref=ref, row=row):
                        at = pl.ds(s * STEP, STEP)
                        into = pl.ds(row + s * STEP, STEP)
                        lane = lo
                        while lane < hi:
                            stop = min(floor_to(lane, LANES) + LANES, hi)
                            if lane % LANES == 0:
                                stop = max(floor_to(hi, LANES), stop)
                            out[into, :, lane:stop] = ref[at, :, lane - base : stop - base]
                            lane = stop
                        return 0

                    lax.fori_loop(0, ref.shape[0] // STEP, plane, 0)
                    row += ref.shape[0]


def per_device(n_band, orbitals):
    orbs, depth, total = orbitals.shape
    chips = n_band // 2
    ranges = Ranges(chips, total)
    index = lax.axis_index("band")
    chip = jnp.stack([index // 2, index % 2]).astype(jnp.int32)
    planes = jnp.transpose(orbitals, (1, 0, 2))

    def along(value, steps):
        pairs = [(i, (i + 2 * steps) % n_band) for i in range(n_band)]
        return lax.ppermute(value, "band", pairs)

    def partner_core(value):
        return lax.ppermute(value, "band", [(i, i ^ 1) for i in range(n_band)])

    n_slab = lax.axis_size("slab")
    up = [(i, (i + 1) % n_slab) for i in range(n_slab)]
    down = [(j, i) for i, j in up]
    below = lax.ppermute(planes[depth - HALO :], "slab", up)
    above = lax.ppermute(planes[:HALO], "slab", down)

    order = [0] + list(range(chips - 1, 0, -1))

    def spread(sent):
        got = [sent[0]]
        for s in range(1, chips):
            got.append(along(sent[s], s))
        return got

    def fetch(pieces):
        sent = pack(ranges, chip, pieces)
        got = spread(sent)
        return [got[s] for s in order]

    inner = depth // CHUNKS
    cut = inner + HALO
    got_a = fetch([(planes, 0, cut)])
    banded = weights(ranges, chip)
    got_low = fetch([(below, 0, HALO)])
    got_b = fetch([(planes, cut, depth), (above, 0, HALO)])
    planes_a = gather([got_low, got_a])

    rows = orbs * chips
    full, swept = (inner + 2 * HALO) * rows, (inner + 2 * REACH) * rows
    work = [
        pltpu.VMEM((2, 2, full, ranges.split_length), jnp.bfloat16),
        pltpu.VMEM((2, full, ranges.full_length), jnp.float32),
        pltpu.VMEM((2, 2, swept, ranges.split_length), jnp.bfloat16),
        pltpu.VMEM((2, swept, ranges.full_length), jnp.float32),
        pltpu.VMEM((4 * swept, TILE), jnp.float32),
        pltpu.VMEM((4 * swept, TILE), jnp.float32),
    ]
    result = sds(inner, rows, ranges.n_second * TILE)
    flops = 8 * WINDOW * TILE * (ranges.n_first + ranges.n_second) * full

    def same(mine, *acc):
        return call(
            functools.partial(same_body, ranges, bool(acc)),
            [result],
            [mine, banded, *acc],
            scratch=work,
            flops=flops,
            limit=12 + 12 * (rows // 8),
        )[0]

    def cross(mine, other, *acc):
        own, travel = call(
            functools.partial(cross_body, ranges, bool(acc)),
            [result, result],
            [chip, mine, banded, other, *acc],
            scratch=work,
            flops=flops,
            smem=True,
            limit=12 + 12 * (rows // 8),
        )
        return own, partner_core(travel)

    def give(acc, back):
        parts = call(
            functools.partial(split_body, ranges),
            [sds(inner, orbs, ranges.out_length)] * chips,
            [chip, acc, back],
            smem=True,
        )
        return spread(parts)

    other_a = partner_core(planes_a)
    acc_a = same(planes_a)
    planes_b = gather([got_b], before=planes_a, kept=2 * HALO, alive=(banded, acc_a))
    other_b = partner_core(planes_b)
    acc_a, back_a = cross(planes_a, other_a, acc_a)
    acc_b, back_b = cross(planes_b, other_b)
    home = give(acc_a, back_a)
    acc_b = same(planes_b, acc_b)
    home += give(acc_b, back_b)
    out = call(
        functools.partial(place_body, ranges), [sds(depth, orbs, total)], [chip, *home], smem=True
    )[0]
    return jnp.transpose(out, (1, 0, 2))


def solution(mesh):
    def body(orbitals):
        return per_device(mesh.shape["band"], orbitals)

    return jax.shard_map(
        body,
        mesh=mesh,
        in_specs=(P("band", "slab", None),),
        out_specs=P("band", "slab", None),
        check_vma=False,
    )
```

```python
import functools

import jax
import jax.numpy as jnp
from jax import lax
from jax.experimental import pallas as pl
from jax.experimental.pallas import tpu as pltpu
from jax.sharding import PartitionSpec as P


NY = 72
LANES = 128
TILE = 256
WINDOW = 3 * TILE
REACH = 2
HALO = 4
CHUNKS = 2
STEP = 2
CENTRE = 8.5
DIAGONAL = 12.0 * CENTRE
SCALE = -1.0 / (CENTRE * DIAGONAL * DIAGONAL)
VMEM = pl.BlockSpec(memory_space=pltpu.VMEM)
SMEM = pl.BlockSpec(memory_space=pltpu.SMEM)


def sds(*shape):
    return jax.ShapeDtypeStruct(shape, jnp.float32)


def call(body, out, inputs, scratch=(), flops=0, smem=False, limit=12):
    nbytes = sum(4 * x.size for x in inputs) + sum(4 * o.size for o in out)
    specs = [VMEM] * len(inputs)
    if smem:
        specs[0] = SMEM
    return pl.pallas_call(
        body,
        out_shape=out,
        in_specs=specs,
        out_specs=[VMEM] * len(out),
        scratch_shapes=scratch,
        compiler_params=pltpu.CompilerParams(vmem_limit_bytes=limit << 20),
        cost_estimate=pl.CostEstimate(flops=flops, bytes_accessed=nbytes, transcendentals=0),
    )(*inputs)


def floor_to(value, unit):
    return value // unit * unit


def ceil_to(value, unit):
    return -(-value // unit) * unit


class Ranges:
    def __init__(self, chips, total):
        self.chips = chips
        self.total = total
        self.width = total // chips
        self.halo = HALO * NY
        starts = [j * self.width - self.halo for j in range(chips)]
        self.starts = [floor_to(s, LANES) for s in starts]
        shifts = [s - a for s, a in zip(starts, self.starts)]
        low, high = min(shifts), max(shifts)
        used = self.width + 2 * self.halo
        self.length = ceil_to(high + used, LANES)
        reach = REACH * NY
        self.first = floor_to(low + reach, LANES)
        self.n_first = ceil_to(high + used - reach - self.first, TILE) // TILE
        self.second = floor_to(low + 2 * reach, LANES)
        self.n_second = ceil_to(high + used - 2 * reach - self.second, TILE) // TILE
        self.out_starts = [floor_to(j * self.width, LANES) for j in range(chips)]
        self.out_length = max(
            ceil_to((j + 1) * self.width, LANES) - s for j, s in enumerate(self.out_starts)
        )

    def shift(self, chip):
        start = chip * self.width - self.halo + ceil_to(self.halo, LANES)
        return lax.rem(start, LANES)

    def out_at(self, chip):
        start = chip * self.width
        return lax.div(start, LANES) * LANES - (start - self.halo - self.shift(chip)) - self.second

    @property
    def pad(self):
        return max(0, TILE - self.first)

    @property
    def split_length(self):
        ends = (
            self.pad + self.first - TILE + self.n_first * TILE + WINDOW - TILE,
            self.pad + self.second - TILE + self.n_second * TILE + WINDOW - TILE,
            self.pad + self.first + self.n_first * TILE,
            self.pad + self.length,
        )
        return ceil_to(max(ends), LANES)

    @property
    def full_length(self):
        return max(
            self.first + self.n_first * TILE, self.second + self.n_second * TILE, self.length
        )


def pack_body(ranges, bounds, chip_ref, *refs):
    chips, total, length = ranges.chips, ranges.total, ranges.length
    ins, outs = refs[:-chips], refs[-chips:]
    chip = chip_ref[0]
    for ahead in range(chips):
        for target in range(chips):

            @pl.when(lax.rem(chip + ahead, chips) == target)
            def _(ahead=ahead, start=ranges.starts[target]):
                row = 0
                for ref, (low, high) in zip(ins, bounds):

                    def plane(s, _, ref=ref, row=row - low, low=low):
                        z = low + s * STEP
                        lo, hi = start, start + length
                        at = pl.ds(z, STEP)
                        pieces = []
                        if lo < 0:
                            pieces.append(ref[at, :, lo + total : total])
                        pieces.append(ref[at, :, max(lo, 0) : min(hi, total)])
                        if hi > total:
                            pieces.append(ref[at, :, 0 : hi - total])
                        value = pieces[0] if len(pieces) == 1 else jnp.concatenate(pieces, axis=-1)
                        outs[ahead][pl.ds(row + z, STEP)] = value
                        return 0

                    lax.fori_loop(0, (high - low) // STEP, plane, 0)
                    row += high - low


def pack(ranges, chip, pieces):
    orbs = pieces[0][0].shape[1]
    bounds = [(low, high) for _, low, high in pieces]
    rows = sum(high - low for low, high in bounds)
    return call(
        functools.partial(pack_body, ranges, bounds),
        [sds(rows, orbs, ranges.length)] * ranges.chips,
        [chip, *(array for array, _, _ in pieces)],
        smem=True,
    )


def gather_body(groups, kept, *refs):
    out = refs[-1]
    row = 0
    if kept:
        before = refs[0]
        out[0:kept] = before[before.shape[0] - kept :]
        refs, row = refs[1:], kept
    slots = (len(refs) - 1) // groups
    for group in range(groups):
        ins = refs[group * slots : (group + 1) * slots]
        orbs = ins[0].shape[1]

        def plane(s, _, ins=ins, row=row):
            z = s * STEP
            for slot, ref in enumerate(ins):
                value = ref[pl.ds(z, STEP)]
                out[pl.ds(row + z, STEP), slot * orbs : (slot + 1) * orbs, :] = value
            return 0

        lax.fori_loop(0, ins[0].shape[0] // STEP, plane, 0)
        row += ins[0].shape[0]


def gather(groups, before=None, kept=0):
    depth = kept + sum(g[0].shape[0] for g in groups)
    _, orbs, span = groups[0][0].shape
    return call(
        functools.partial(gather_body, len(groups), kept),
        [sds(depth, orbs * len(groups[0]), span)],
        [*([before] if kept else []), *(p for g in groups for p in g)],
    )[0]


def roll_rows(value, shift):
    if isinstance(shift, int):
        shift = shift % value.shape[1]
        if shift == 0:
            return value
    return pltpu.roll(value, shift, 1)


class Pairing:
    def __init__(self, rows, even, odd=None):
        self.rows, self.even, self.odd = rows, even, odd

    def apply(self, value, even, odd):
        if odd is None:
            return roll_rows(value, even)
        row = lax.broadcasted_iota(jnp.int32, value.shape, 1)
        return jnp.where(row % 2 == 0, roll_rows(value, even), roll_rows(value, odd))

    def negative(self, shift):
        return -shift if isinstance(shift, int) else lax.rem(self.rows - shift, self.rows)

    def partner(self, value):
        return self.apply(value, self.even, self.odd)

    def back(self, value):
        if self.odd is None:
            return self.apply(value, self.negative(self.even), None)
        return self.apply(value, self.negative(self.odd), self.negative(self.even))


def weights_body(ranges, chip_ref, out):
    i = lax.broadcasted_iota(jnp.int32, (WINDOW, TILE), 0)
    lane = lax.broadcasted_iota(jnp.int32, (1, TILE), 1)
    shift = ranges.shift(chip_ref[0])
    at = lane + TILE

    def tile(t, start, diagonal):
        y = lax.rem(lane + (start + 2 * NY) - shift, NY)
        near = (i == at - NY) | (i == at + NY)
        far = (i == at - 2 * NY) | (i == at + 2 * NY)

        def beside(step):
            wrap = jnp.where(y + step >= NY, NY, jnp.where(y + step < 0, -NY, 0))
            return i == at + step - wrap

        near = near | beside(1) | beside(-1)
        far = far | beside(2) | beside(-2)
        value = jnp.where(i == at, diagonal, 0.0)
        value = jnp.where(near, 16.0, jnp.where(far, -1.0, value))
        out[t] = value.astype(jnp.bfloat16)

    def first(t, _):
        tile(t, ranges.first + t * TILE, DIAGONAL)
        return 0

    def second(t, _):
        tile(ranges.n_first + t, ranges.second + t * TILE, 0.0)
        return 0

    lax.fori_loop(0, ranges.n_first, first, 0)
    lax.fori_loop(0, ranges.n_second, second, 0)


def weights(ranges, chip):
    shape = (ranges.n_first + ranges.n_second, WINDOW, TILE)
    out = jax.ShapeDtypeStruct(shape, jnp.bfloat16)
    return call(functools.partial(weights_body, ranges), [out], [chip], smem=True)[0]


def store_halves(ref, rows, lanes, value):
    high = value.astype(jnp.bfloat16)
    ref[0, rows, lanes] = high
    ref[1, rows, lanes] = (value - high.astype(jnp.float32)).astype(jnp.bfloat16)


def aligned(start, size):
    if isinstance(start, int):
        return slice(start, start + size)
    return pl.ds(pl.multiple_of(start, LANES), size)


def potentials(ranges, first, seconds, pairings, w_ref, work, finish):
    rho_split, rho, mid_split, mid, *products = work
    depth, n_rows, span = first.shape
    inner = depth - 2 * HALO
    swept = inner + 2 * REACH
    pad = ranges.pad
    kinds = len(seconds)

    def density(s, _):
        planes = pl.ds(s * STEP, STEP)
        rows = pl.ds(pl.multiple_of(s * (STEP * n_rows), STEP * n_rows), STEP * n_rows)
        for lo in range(0, span, LANES):
            lanes = slice(lo, lo + LANES)
            mine = first[planes, :, lanes]
            for k, (second, pairing) in enumerate(zip(seconds, pairings)):
                value = mine * pairing.partner(second[planes, :, lanes])
                value = value.reshape(STEP * n_rows, LANES)
                store_halves(rho_split.at[k], rows, slice(lo + pad, lo + pad + LANES), value)
                rho[k, rows, lanes] = value
        return 0

    lax.fori_loop(0, depth // STEP, density, 0)

    def in_plane(source, planes, start, weight, product):
        lanes = aligned(start - TILE + pad, WINDOW)
        rows = planes * n_rows
        value = source[:, :, REACH * n_rows : REACH * n_rows + rows, lanes]
        value = value.reshape(2 * kinds * rows, WINDOW)
        product[0 : 2 * kinds * rows] = jnp.dot(value, weight, preferred_element_type=jnp.float32)

    def off(source, k, planes, start, product):
        rows = planes * n_rows

        def shifted(z):
            return source[k, z * n_rows : z * n_rows + rows, aligned(start, TILE)]

        near = shifted(1) + shifted(3)
        far = shifted(0) + shifted(4)
        row = 2 * k * rows
        inside = product[row : row + rows] + product[row + rows : row + 2 * rows]
        return inside + (16.0 * near - far)

    def pipelined(count, multiply, use):
        multiply(0, products[0])
        for t in range(count):
            if t + 1 < count:
                multiply(t + 1, products[(t + 1) % 2])
            use(t, products[t % 2])

    def multiply_1(t, product):
        in_plane(rho_split, swept, ranges.first + t * TILE, w_ref[t], product)

    def use_1(t, product):
        start = ranges.first + t * TILE
        for k in range(kinds):
            value = off(rho, k, swept, start, product)
            mid[k, :, aligned(start, TILE)] = value
            store_halves(mid_split.at[k], slice(None), aligned(start + pad, TILE), value)

    pipelined(ranges.n_first, multiply_1, use_1)

    def multiply_2(t, product):
        start = ranges.second + t * TILE
        in_plane(mid_split, inner, start, w_ref[t + ranges.n_first], product)

    def use_2(t, product):
        start = ranges.second + t * TILE
        here = aligned(start, TILE)
        values = []
        for k in range(kinds):
            value = off(mid, k, inner, start, product)
            source = rho[k, HALO * n_rows : (HALO + inner) * n_rows, here]
            value = value + (DIAGONAL * DIAGONAL) * source
            values.append(value.reshape(inner, n_rows, TILE))
        finish(here, aligned(t * TILE, TILE), values)

    pipelined(ranges.n_second, multiply_2, use_2)


def clear(ranges, work):
    rho_split, rho, mid_split, mid = work[:4]
    span = ranges.length

    def zero(ref, lo, hi):
        if lo < hi:
            shape = ref.shape[:-1] + (hi - lo,)
            ref[..., lo:hi] = jnp.zeros(shape, ref.dtype)

    pad, end = ranges.pad, ranges.split_length
    zero(rho_split, 0, pad)
    zero(rho_split, pad + span, end)
    zero(rho, span, rho.shape[-1])
    zero(mid_split, 0, pad + ranges.first)
    zero(mid_split, pad + ranges.first + ranges.n_first * TILE, end)
    zero(mid, 0, ranges.first)
    zero(mid, ranges.first + ranges.n_first * TILE, mid.shape[-1])


def total_of(acc_in, lanes, total):
    return total if acc_in is None else (total + acc_in[:, :, lanes]) * SCALE


def same_body(ranges, follows, planes, w_ref, *refs):
    acc_in = refs[0] if follows else None
    acc, *work = refs[1:] if follows else refs
    depth, n_rows, _ = planes.shape
    inner = slice(HALO, depth - HALO)
    pairings = (Pairing(n_rows, 2), Pairing(n_rows, 1, 3))

    def finish(here, lanes, values):
        mine = planes[inner, :, here]
        total = None
        for value, pairing in zip(values, pairings):
            part = value * pairing.partner(mine) + pairing.back(value * mine)
            total = part if total is None else total + part
        acc[:, :, lanes] = total_of(acc_in, lanes, total)

    clear(ranges, work)
    potentials(ranges, planes, (planes, planes), pairings, w_ref, work, finish)


def cross_body(ranges, follows, chip_ref, planes, w_ref, other, *refs):
    acc_in = refs[0] if follows else None
    acc, travel, *work = refs[1:] if follows else refs
    depth, n_rows, _ = planes.shape
    inner = slice(HALO, depth - HALO)
    odd = chip_ref[1] == 1
    pairings = (
        Pairing(n_rows, jnp.where(odd, 0, 2)),
        Pairing(n_rows, jnp.where(odd, n_rows - 1, 1), jnp.where(odd, 1, 3)),
    )

    def finish(here, lanes, values):
        mine, theirs = planes[inner, :, here], other[inner, :, here]
        own = away = None
        for value, pairing in zip(values, pairings):
            to_own = value * pairing.partner(theirs)
            to_away = pairing.back(value * mine)
            own = to_own if own is None else own + to_own
            away = to_away if away is None else away + to_away
        acc[:, :, lanes] = total_of(acc_in, lanes, own)
        travel[:, :, lanes] = away * SCALE

    clear(ranges, work)
    potentials(ranges, planes, (other, other), pairings, w_ref, work, finish)


def split_body(ranges, chip_ref, mine, theirs, *outs):
    orbs = outs[0].shape[1]
    lanes = aligned(ranges.out_at(chip_ref[0]), ranges.out_length)

    def plane(s, _):
        at = pl.ds(s * STEP, STEP)
        value = mine[at, :, lanes] + theirs[at, :, lanes]
        for slot, out in enumerate(outs):
            out[at] = value[:, slot * orbs : (slot + 1) * orbs]
        return 0

    lax.fori_loop(0, outs[0].shape[0] // STEP, plane, 0)


def place_body(ranges, chip_ref, *refs):
    chips = ranges.chips
    ins, out = refs[:-1], refs[-1]
    chip = chip_ref[0]
    for behind in range(chips):
        for source in range(chips):

            @pl.when(lax.rem(chip + chips - behind, chips) == source)
            def _(parts=ins[behind::chips], source=source):
                base = ranges.out_starts[source]
                lo, hi = source * ranges.width, (source + 1) * ranges.width
                row = 0
                for ref in parts:

                    def plane(s, _, ref=ref, row=row):
                        at = pl.ds(s * STEP, STEP)
                        into = pl.ds(row + s * STEP, STEP)
                        lane = lo
                        while lane < hi:
                            stop = min(floor_to(lane, LANES) + LANES, hi)
                            if lane % LANES == 0:
                                stop = max(floor_to(hi, LANES), stop)
                            out[into, :, lane:stop] = ref[at, :, lane - base : stop - base]
                            lane = stop
                        return 0

                    lax.fori_loop(0, ref.shape[0] // STEP, plane, 0)
                    row += ref.shape[0]


def per_device(n_band, orbitals):
    orbs, depth, total = orbitals.shape
    chips = n_band // 2
    ranges = Ranges(chips, total)
    index = lax.axis_index("band")
    chip = jnp.stack([index // 2, index % 2]).astype(jnp.int32)
    planes = jnp.transpose(orbitals, (1, 0, 2))

    def along(value, steps):
        pairs = [(i, (i + 2 * steps) % n_band) for i in range(n_band)]
        return lax.ppermute(value, "band", pairs)

    def partner_core(value):
        return lax.ppermute(value, "band", [(i, i ^ 1) for i in range(n_band)])

    n_slab = lax.axis_size("slab")
    up = [(i, (i + 1) % n_slab) for i in range(n_slab)]
    down = [(j, i) for i, j in up]
    below = lax.ppermute(planes[depth - HALO :], "slab", up)
    above = lax.ppermute(planes[:HALO], "slab", down)

    order = [0] + list(range(chips - 1, 0, -1))

    def spread(sent):
        got = [sent[0]]
        for s in range(1, chips):
            got.append(along(sent[s], s))
        return got

    def fetch(pieces):
        sent = pack(ranges, chip, pieces)
        got = spread(sent)
        return [got[s] for s in order]

    inner = depth // CHUNKS
    cut = inner + HALO
    got_a = fetch([(planes, 0, cut)])
    banded = weights(ranges, chip)
    got_low = fetch([(below, 0, HALO)])
    got_b = fetch([(planes, cut, depth), (above, 0, HALO)])
    planes_a = gather([got_low, got_a])

    rows = orbs * chips
    full, swept = (inner + 2 * HALO) * rows, (inner + 2 * REACH) * rows
    work = [
        pltpu.VMEM((2, 2, full, ranges.split_length), jnp.bfloat16),
        pltpu.VMEM((2, full, ranges.full_length), jnp.float32),
        pltpu.VMEM((2, 2, swept, ranges.split_length), jnp.bfloat16),
        pltpu.VMEM((2, swept, ranges.full_length), jnp.float32),
        pltpu.VMEM((4 * swept, TILE), jnp.float32),
        pltpu.VMEM((4 * swept, TILE), jnp.float32),
    ]
    result = sds(inner, rows, ranges.n_second * TILE)
    flops = 8 * WINDOW * TILE * (ranges.n_first + ranges.n_second) * full

    def same(mine, *acc):
        return call(
            functools.partial(same_body, ranges, bool(acc)),
            [result],
            [mine, banded, *acc],
            scratch=work,
            flops=flops,
            limit=12 + 12 * (rows // 8),
        )[0]

    def cross(mine, other, *acc):
        own, travel = call(
            functools.partial(cross_body, ranges, bool(acc)),
            [result, result],
            [chip, mine, banded, other, *acc],
            scratch=work,
            flops=flops,
            smem=True,
            limit=12 + 12 * (rows // 8),
        )
        return own, partner_core(travel)

    def give(acc, back):
        parts = call(
            functools.partial(split_body, ranges),
            [sds(inner, orbs, ranges.out_length)] * chips,
            [chip, acc, back],
            smem=True,
        )
        return spread(parts)

    other_a = partner_core(planes_a)
    acc_a = same(planes_a)
    acc_a, back_a = cross(planes_a, other_a, acc_a)
    planes_b = gather([got_b], before=planes_a, kept=2 * HALO)
    other_b = partner_core(planes_b)
    home = give(acc_a, back_a)
    acc_b, back_b = cross(planes_b, other_b)
    acc_b = same(planes_b, acc_b)
    home += give(acc_b, back_b)
    out = call(
        functools.partial(place_body, ranges), [sds(depth, orbs, total)], [chip, *home], smem=True
    )[0]
    return jnp.transpose(out, (1, 0, 2))


def solution(mesh):
    def body(orbitals):
        return per_device(mesh.shape["band"], orbitals)

    return jax.shard_map(
        body,
        mesh=mesh,
        in_specs=(P("band", "slab", None),),
        out_specs=P("band", "slab", None),
        check_vma=False,
    )
```

```python
import functools

import jax
import jax.numpy as jnp
from jax import lax
from jax.experimental import pallas as pl
from jax.experimental.pallas import tpu as pltpu
from jax.sharding import PartitionSpec as P


NY = 72
LANES = 128
TILE = 256
WINDOW = 3 * TILE
REACH = 2
HALO = 4
CHUNKS = 2
STEP = 2
CENTRE = 8.5
DIAGONAL = 12.0 * CENTRE
SCALE = -1.0 / (CENTRE * DIAGONAL * DIAGONAL)
VMEM = pl.BlockSpec(memory_space=pltpu.VMEM)
SMEM = pl.BlockSpec(memory_space=pltpu.SMEM)


def sds(*shape):
    return jax.ShapeDtypeStruct(shape, jnp.float32)


def call(body, out, inputs, scratch=(), flops=0, smem=False, limit=12):
    nbytes = sum(4 * x.size for x in inputs) + sum(4 * o.size for o in out)
    specs = [VMEM] * len(inputs)
    if smem:
        specs[0] = SMEM
    return pl.pallas_call(
        body,
        out_shape=out,
        in_specs=specs,
        out_specs=[VMEM] * len(out),
        scratch_shapes=scratch,
        compiler_params=pltpu.CompilerParams(vmem_limit_bytes=limit << 20),
        cost_estimate=pl.CostEstimate(flops=flops, bytes_accessed=nbytes, transcendentals=0),
    )(*inputs)


def floor_to(value, unit):
    return value // unit * unit


def ceil_to(value, unit):
    return -(-value // unit) * unit


def on_each_chip(chip, chips, body):
    for index in range(chips):
        pl.when(chip == index)(functools.partial(body, index))


def peer(index, turn, chips, sending):
    if chips & (chips - 1) == 0:
        return index ^ turn
    return (index + (turn if sending else -turn)) % chips


class Ranges:
    def __init__(self, chips, total):
        self.chips = chips
        self.total = total
        self.width = total // chips
        self.halo = HALO * NY
        starts = [j * self.width - self.halo for j in range(chips)]
        self.starts = [floor_to(s, LANES) for s in starts]
        shifts = [s - a for s, a in zip(starts, self.starts)]
        low, high = min(shifts), max(shifts)
        used = self.width + 2 * self.halo
        self.length = ceil_to(high + used, LANES)
        reach = REACH * NY
        self.first = floor_to(low + reach, LANES)
        self.n_first = ceil_to(high + used - reach - self.first, TILE) // TILE
        self.second = floor_to(low + 2 * reach, LANES)
        self.n_second = ceil_to(high + used - 2 * reach - self.second, TILE) // TILE
        self.out_starts = [floor_to(j * self.width, LANES) for j in range(chips)]
        self.out_length = max(
            ceil_to((j + 1) * self.width, LANES) - s for j, s in enumerate(self.out_starts)
        )

    def shift(self, chip):
        start = chip * self.width - self.halo + ceil_to(self.halo, LANES)
        return lax.rem(start, LANES)

    def out_at(self, chip):
        start = chip * self.width
        return lax.div(start, LANES) * LANES - (start - self.halo - self.shift(chip)) - self.second

    @property
    def pad(self):
        return max(0, TILE - self.first)

    @property
    def split_length(self):
        ends = (
            self.pad + self.first - TILE + self.n_first * TILE + WINDOW - TILE,
            self.pad + self.second - TILE + self.n_second * TILE + WINDOW - TILE,
            self.pad + self.first + self.n_first * TILE,
            self.pad + self.length,
        )
        return ceil_to(max(ends), LANES)

    @property
    def full_length(self):
        return max(
            self.first + self.n_first * TILE, self.second + self.n_second * TILE, self.length
        )


def pack_body(ranges, bounds, chip_ref, *refs):
    chips, total, length = ranges.chips, ranges.total, ranges.length
    ins, outs = refs[:-chips], refs[-chips:]

    def cut(ref, at, lo, hi):
        pieces = []
        if lo < 0:
            pieces.append(ref[at, :, lo + total : total])
        pieces.append(ref[at, :, max(lo, 0) : min(hi, total)])
        if hi > total:
            pieces.append(ref[at, :, 0 : hi - total])
        return pieces[0] if len(pieces) == 1 else jnp.concatenate(pieces, axis=-1)

    def body(index):
        row = 0
        for ref, (low, high) in zip(ins, bounds):

            def plane(s, _, ref=ref, row=row - low, low=low):
                z = low + s * STEP
                for turn in range(chips):
                    start = ranges.starts[peer(index, turn, chips, True)]
                    value = cut(ref, pl.ds(z, STEP), start, start + length)
                    outs[turn][pl.ds(row + z, STEP)] = value
                return 0

            lax.fori_loop(0, (high - low) // STEP, plane, 0)
            row += high - low

    on_each_chip(chip_ref[0], chips, body)


def pack(ranges, chip, pieces):
    orbs = pieces[0][0].shape[1]
    bounds = [(low, high) for _, low, high in pieces]
    rows = sum(high - low for low, high in bounds)
    return call(
        functools.partial(pack_body, ranges, bounds),
        [sds(rows, orbs, ranges.length)] * ranges.chips,
        [chip, *(array for array, _, _ in pieces)],
        smem=True,
    )


def gather_body(groups, kept, chips, chip_ref, *refs):
    out = refs[-1]
    if kept:
        before = refs[0]
        out[0:kept] = before[before.shape[0] - kept :]
        refs = refs[1:]

    def body(index):
        row = kept
        for group in range(groups):
            ins = refs[group * chips : (group + 1) * chips]
            orbs = ins[0].shape[1]

            def plane(s, _, ins=ins, row=row):
                z = s * STEP
                for turn, ref in enumerate(ins):
                    slot = (peer(index, turn, chips, False) - index) % chips
                    value = ref[pl.ds(z, STEP)]
                    out[pl.ds(row + z, STEP), slot * orbs : (slot + 1) * orbs, :] = value
                return 0

            lax.fori_loop(0, ins[0].shape[0] // STEP, plane, 0)
            row += ins[0].shape[0]

    on_each_chip(chip_ref[0], chips, body)


def gather(chip, groups, before=None, kept=0):
    depth = kept + sum(g[0].shape[0] for g in groups)
    _, orbs, span = groups[0][0].shape
    chips = len(groups[0])
    return call(
        functools.partial(gather_body, len(groups), kept, chips),
        [sds(depth, orbs * chips, span)],
        [chip, *([before] if kept else []), *(p for g in groups for p in g)],
        smem=True,
    )[0]


def roll_rows(value, shift):
    if isinstance(shift, int):
        shift = shift % value.shape[1]
        if shift == 0:
            return value
    return pltpu.roll(value, shift, 1)


class Pairing:
    def __init__(self, rows, even, odd=None):
        self.rows, self.even, self.odd = rows, even, odd

    def apply(self, value, even, odd):
        if odd is None:
            return roll_rows(value, even)
        row = lax.broadcasted_iota(jnp.int32, value.shape, 1)
        return jnp.where(row % 2 == 0, roll_rows(value, even), roll_rows(value, odd))

    def negative(self, shift):
        return -shift if isinstance(shift, int) else lax.rem(self.rows - shift, self.rows)

    def partner(self, value):
        return self.apply(value, self.even, self.odd)

    def back(self, value):
        if self.odd is None:
            return self.apply(value, self.negative(self.even), None)
        return self.apply(value, self.negative(self.odd), self.negative(self.even))


def weights_body(ranges, chip_ref, out):
    i = lax.broadcasted_iota(jnp.int32, (WINDOW, TILE), 0)
    lane = lax.broadcasted_iota(jnp.int32, (1, TILE), 1)
    shift = ranges.shift(chip_ref[0])
    at = lane + TILE

    def tile(t, start, diagonal):
        y = lax.rem(lane + (start + 2 * NY) - shift, NY)
        near = (i == at - NY) | (i == at + NY)
        far = (i == at - 2 * NY) | (i == at + 2 * NY)

        def beside(step):
            wrap = jnp.where(y + step >= NY, NY, jnp.where(y + step < 0, -NY, 0))
            return i == at + step - wrap

        near = near | beside(1) | beside(-1)
        far = far | beside(2) | beside(-2)
        value = jnp.where(i == at, diagonal, 0.0)
        value = jnp.where(near, 16.0, jnp.where(far, -1.0, value))
        out[t] = value.astype(jnp.bfloat16)

    def first(t, _):
        tile(t, ranges.first + t * TILE, DIAGONAL)
        return 0

    def second(t, _):
        tile(ranges.n_first + t, ranges.second + t * TILE, 0.0)
        return 0

    lax.fori_loop(0, ranges.n_first, first, 0)
    lax.fori_loop(0, ranges.n_second, second, 0)


def weights(ranges, chip):
    shape = (ranges.n_first + ranges.n_second, WINDOW, TILE)
    out = jax.ShapeDtypeStruct(shape, jnp.bfloat16)
    return call(functools.partial(weights_body, ranges), [out], [chip], smem=True)[0]


def store_halves(ref, rows, lanes, value):
    high = value.astype(jnp.bfloat16)
    ref[0, rows, lanes] = high
    ref[1, rows, lanes] = (value - high.astype(jnp.float32)).astype(jnp.bfloat16)


def aligned(start, size):
    if isinstance(start, int):
        return slice(start, start + size)
    return pl.ds(pl.multiple_of(start, LANES), size)


def potentials(ranges, first, seconds, pairings, w_ref, work, finish):
    rho_split, rho, mid_split, mid, *products = work
    depth, n_rows, span = first.shape
    inner = depth - 2 * HALO
    swept = inner + 2 * REACH
    pad = ranges.pad
    kinds = len(seconds)

    def density(s, _):
        planes = pl.ds(s * STEP, STEP)
        rows = pl.ds(pl.multiple_of(s * (STEP * n_rows), STEP * n_rows), STEP * n_rows)
        for lo in range(0, span, LANES):
            lanes = slice(lo, lo + LANES)
            mine = first[planes, :, lanes]
            for k, (second, pairing) in enumerate(zip(seconds, pairings)):
                value = mine * pairing.partner(second[planes, :, lanes])
                value = value.reshape(STEP * n_rows, LANES)
                store_halves(rho_split.at[k], rows, slice(lo + pad, lo + pad + LANES), value)
                rho[k, rows, lanes] = value
        return 0

    lax.fori_loop(0, depth // STEP, density, 0)

    def in_plane(source, planes, start, weight, product):
        lanes = aligned(start - TILE + pad, WINDOW)
        rows = planes * n_rows
        value = source[:, :, REACH * n_rows : REACH * n_rows + rows, lanes]
        value = value.reshape(2 * kinds * rows, WINDOW)
        product[0 : 2 * kinds * rows] = jnp.dot(value, weight, preferred_element_type=jnp.float32)

    def off(source, k, planes, start, product):
        rows = planes * n_rows

        def shifted(z):
            return source[k, z * n_rows : z * n_rows + rows, aligned(start, TILE)]

        near = shifted(1) + shifted(3)
        far = shifted(0) + shifted(4)
        row = 2 * k * rows
        inside = product[row : row + rows] + product[row + rows : row + 2 * rows]
        return inside + (16.0 * near - far)

    def pipelined(count, multiply, use):
        multiply(0, products[0])
        for t in range(count):
            if t + 1 < count:
                multiply(t + 1, products[(t + 1) % 2])
            use(t, products[t % 2])

    def multiply_1(t, product):
        in_plane(rho_split, swept, ranges.first + t * TILE, w_ref[t], product)

    def use_1(t, product):
        start = ranges.first + t * TILE
        for k in range(kinds):
            value = off(rho, k, swept, start, product)
            mid[k, :, aligned(start, TILE)] = value
            store_halves(mid_split.at[k], slice(None), aligned(start + pad, TILE), value)

    pipelined(ranges.n_first, multiply_1, use_1)

    def multiply_2(t, product):
        start = ranges.second + t * TILE
        in_plane(mid_split, inner, start, w_ref[t + ranges.n_first], product)

    def use_2(t, product):
        start = ranges.second + t * TILE
        here = aligned(start, TILE)
        values = []
        for k in range(kinds):
            value = off(mid, k, inner, start, product)
            source = rho[k, HALO * n_rows : (HALO + inner) * n_rows, here]
            value = value + (DIAGONAL * DIAGONAL) * source
            values.append(value.reshape(inner, n_rows, TILE))
        finish(here, aligned(t * TILE, TILE), values)

    pipelined(ranges.n_second, multiply_2, use_2)


def clear(ranges, work):
    rho_split, rho, mid_split, mid = work[:4]
    span = ranges.length

    def zero(ref, lo, hi):
        if lo < hi:
            shape = ref.shape[:-1] + (hi - lo,)
            ref[..., lo:hi] = jnp.zeros(shape, ref.dtype)

    pad, end = ranges.pad, ranges.split_length
    zero(rho_split, 0, pad)
    zero(rho_split, pad + span, end)
    zero(rho, span, rho.shape[-1])
    zero(mid_split, 0, pad + ranges.first)
    zero(mid_split, pad + ranges.first + ranges.n_first * TILE, end)
    zero(mid, 0, ranges.first)
    zero(mid, ranges.first + ranges.n_first * TILE, mid.shape[-1])


def total_of(acc_in, lanes, total):
    return total if acc_in is None else (total + acc_in[:, :, lanes]) * SCALE


def same_body(ranges, follows, planes, w_ref, *refs):
    acc_in = refs[0] if follows else None
    acc, *work = refs[1:] if follows else refs
    depth, n_rows, _ = planes.shape
    inner = slice(HALO, depth - HALO)
    pairings = (Pairing(n_rows, 2), Pairing(n_rows, 1, 3))

    def finish(here, lanes, values):
        mine = planes[inner, :, here]
        total = None
        for value, pairing in zip(values, pairings):
            part = value * pairing.partner(mine) + pairing.back(value * mine)
            total = part if total is None else total + part
        acc[:, :, lanes] = total_of(acc_in, lanes, total)

    clear(ranges, work)
    potentials(ranges, planes, (planes, planes), pairings, w_ref, work, finish)


def cross_body(ranges, follows, chip_ref, planes, w_ref, other, *refs):
    acc_in = refs[0] if follows else None
    acc, travel, *work = refs[1:] if follows else refs
    depth, n_rows, _ = planes.shape
    inner = slice(HALO, depth - HALO)
    odd = chip_ref[1] == 1
    pairings = (
        Pairing(n_rows, jnp.where(odd, 0, 2)),
        Pairing(n_rows, jnp.where(odd, n_rows - 1, 1), jnp.where(odd, 1, 3)),
    )

    def finish(here, lanes, values):
        mine, theirs = planes[inner, :, here], other[inner, :, here]
        own = away = None
        for value, pairing in zip(values, pairings):
            to_own = value * pairing.partner(theirs)
            to_away = pairing.back(value * mine)
            own = to_own if own is None else own + to_own
            away = to_away if away is None else away + to_away
        acc[:, :, lanes] = total_of(acc_in, lanes, own)
        travel[:, :, lanes] = away * SCALE

    clear(ranges, work)
    potentials(ranges, planes, (other, other), pairings, w_ref, work, finish)


def split_body(ranges, chip_ref, mine, theirs, *outs):
    orbs = outs[0].shape[1]
    lanes = aligned(ranges.out_at(chip_ref[0]), ranges.out_length)

    def body(index):
        def plane(s, _):
            at = pl.ds(s * STEP, STEP)
            value = mine[at, :, lanes] + theirs[at, :, lanes]
            for turn, out in enumerate(outs):
                slot = (peer(index, turn, ranges.chips, True) - index) % ranges.chips
                out[at] = value[:, slot * orbs : (slot + 1) * orbs]
            return 0

        lax.fori_loop(0, outs[0].shape[0] // STEP, plane, 0)

    on_each_chip(chip_ref[0], ranges.chips, body)


def place_body(ranges, chip_ref, *refs):
    chips = ranges.chips
    ins, out = refs[:-1], refs[-1]

    def body(index):
        row = 0
        for first in range(0, len(ins), chips):

            def plane(s, _, row=row, first=first):
                at = pl.ds(s * STEP, STEP)
                into = pl.ds(row + s * STEP, STEP)
                for turn in range(chips):
                    source = peer(index, turn, chips, False)
                    base = ranges.out_starts[source]
                    lane, hi = source * ranges.width, (source + 1) * ranges.width
                    while lane < hi:
                        stop = min(floor_to(lane, LANES) + LANES, hi)
                        if lane % LANES == 0:
                            stop = max(floor_to(hi, LANES), stop)
                        out[into, :, lane:stop] = ins[first + turn][at, :, lane - base : stop - base]
                        lane = stop
                return 0

            lax.fori_loop(0, ins[first].shape[0] // STEP, plane, 0)
            row += ins[first].shape[0]

    on_each_chip(chip_ref[0], chips, body)


def per_device(n_band, orbitals):
    orbs, depth, total = orbitals.shape
    chips = n_band // 2
    ranges = Ranges(chips, total)
    index = lax.axis_index("band")
    chip = jnp.stack([index // 2, index % 2]).astype(jnp.int32)
    planes = jnp.transpose(orbitals, (1, 0, 2))

    def exchange(value, turn):
        pairs = [(i, peer(i // 2, turn, chips, True) * 2 + i % 2) for i in range(n_band)]
        return lax.ppermute(value, "band", pairs)

    def partner_core(value):
        return lax.ppermute(value, "band", [(i, i ^ 1) for i in range(n_band)])

    n_slab = lax.axis_size("slab")
    up = [(i, (i + 1) % n_slab) for i in range(n_slab)]
    down = [(j, i) for i, j in up]
    below = lax.ppermute(planes[depth - HALO :], "slab", up)
    above = lax.ppermute(planes[:HALO], "slab", down)

    def spread(sent):
        got = [sent[0]]
        for turn in range(1, chips):
            got.append(exchange(sent[turn], turn))
        return got

    def fetch(pieces):
        sent = pack(ranges, chip, pieces)
        return spread(sent)

    inner = depth // CHUNKS
    cut = inner + HALO
    got_a = fetch([(planes, 0, cut)])
    banded = weights(ranges, chip)
    got_low = fetch([(below, 0, HALO)])
    got_b = fetch([(planes, cut, depth), (above, 0, HALO)])
    planes_a = gather(chip, [got_low, got_a])

    rows = orbs * chips
    full, swept = (inner + 2 * HALO) * rows, (inner + 2 * REACH) * rows
    work = [
        pltpu.VMEM((2, 2, full, ranges.split_length), jnp.bfloat16),
        pltpu.VMEM((2, full, ranges.full_length), jnp.float32),
        pltpu.VMEM((2, 2, swept, ranges.split_length), jnp.bfloat16),
        pltpu.VMEM((2, swept, ranges.full_length), jnp.float32),
        pltpu.VMEM((4 * swept, TILE), jnp.float32),
        pltpu.VMEM((4 * swept, TILE), jnp.float32),
    ]
    result = sds(inner, rows, ranges.n_second * TILE)
    flops = 8 * WINDOW * TILE * (ranges.n_first + ranges.n_second) * full

    def same(mine, *acc):
        return call(
            functools.partial(same_body, ranges, bool(acc)),
            [result],
            [mine, banded, *acc],
            scratch=work,
            flops=flops,
            limit=12 + 12 * (rows // 8),
        )[0]

    def cross(mine, other, *acc):
        own, travel = call(
            functools.partial(cross_body, ranges, bool(acc)),
            [result, result],
            [chip, mine, banded, other, *acc],
            scratch=work,
            flops=flops,
            smem=True,
            limit=12 + 12 * (rows // 8),
        )
        return own, partner_core(travel)

    def give(acc, back):
        parts = call(
            functools.partial(split_body, ranges),
            [sds(inner, orbs, ranges.out_length)] * chips,
            [chip, acc, back],
            smem=True,
        )
        return spread(parts)

    other_a = partner_core(planes_a)
    acc_a = same(planes_a)
    acc_a, back_a = cross(planes_a, other_a, acc_a)
    planes_b = gather(chip, [got_b], before=planes_a, kept=2 * HALO)
    other_b = partner_core(planes_b)
    home = give(acc_a, back_a)
    acc_b, back_b = cross(planes_b, other_b)
    acc_b = same(planes_b, acc_b)
    home += give(acc_b, back_b)
    out = call(
        functools.partial(place_body, ranges), [sds(depth, orbs, total)], [chip, *home], smem=True
    )[0]
    return jnp.transpose(out, (1, 0, 2))


def solution(mesh):
    def body(orbitals):
        return per_device(mesh.shape["band"], orbitals)

    return jax.shard_map(
        body,
        mesh=mesh,
        in_specs=(P("band", "slab", None),),
        out_specs=P("band", "slab", None),
        check_vma=False,
    )
```

```python
import functools

import jax
import jax.numpy as jnp
from jax import lax
from jax.experimental import pallas as pl
from jax.experimental.pallas import tpu as pltpu
from jax.sharding import PartitionSpec as P


NY = 72
LANES = 128
TILE = 256
WINDOW = 2 * TILE
REACH = 2
HALO = 4
CHUNKS = 2
STEP = 2
CENTRE = 8.5
DIAGONAL = 12.0 * CENTRE
SCALE = -1.0 / (CENTRE * DIAGONAL * DIAGONAL)
VMEM = pl.BlockSpec(memory_space=pltpu.VMEM)
SMEM = pl.BlockSpec(memory_space=pltpu.SMEM)


def sds(*shape):
    return jax.ShapeDtypeStruct(shape, jnp.float32)


def call(body, out, inputs, scratch=(), flops=0, smem=False, limit=12):
    nbytes = sum(4 * x.size for x in inputs) + sum(4 * o.size for o in out)
    specs = [VMEM] * len(inputs)
    if smem:
        specs[0] = SMEM
    return pl.pallas_call(
        body,
        out_shape=out,
        in_specs=specs,
        out_specs=[VMEM] * len(out),
        scratch_shapes=scratch,
        compiler_params=pltpu.CompilerParams(vmem_limit_bytes=limit << 20),
        cost_estimate=pl.CostEstimate(flops=flops, bytes_accessed=nbytes, transcendentals=0),
    )(*inputs)


def floor_to(value, unit):
    return value // unit * unit


def ceil_to(value, unit):
    return -(-value // unit) * unit


def on_each_chip(chip, chips, body):
    for index in range(chips):
        pl.when(chip == index)(functools.partial(body, index))


def peer(index, turn, chips, sending):
    if chips & (chips - 1) == 0:
        return index ^ turn
    return (index + (turn if sending else -turn)) % chips


class Ranges:
    def __init__(self, chips, total):
        self.chips = chips
        self.total = total
        self.width = total // chips
        self.halo = HALO * NY
        starts = [j * self.width - self.halo for j in range(chips)]
        self.starts = [floor_to(s, LANES) for s in starts]
        shifts = [s - a for s, a in zip(starts, self.starts)]
        low, high = min(shifts), max(shifts)
        used = self.width + 2 * self.halo
        self.length = ceil_to(high + used, LANES)
        reach = REACH * NY
        self.first = floor_to(low + reach, LANES)
        self.n_first = ceil_to(high + used - reach - self.first, TILE) // TILE
        self.second = floor_to(low + 2 * reach, LANES)
        self.n_second = ceil_to(high + used - 2 * reach - self.second, TILE) // TILE
        self.needed = [(low + n * reach, high + used - n * reach) for n in (1, 2)]
        self.out_starts = [floor_to(j * self.width, LANES) for j in range(chips)]
        self.out_length = max(
            ceil_to((j + 1) * self.width, LANES) - s for j, s in enumerate(self.out_starts)
        )

    def shift(self, chip):
        start = chip * self.width - self.halo + ceil_to(self.halo, LANES)
        return lax.rem(start, LANES)

    def out_at(self, chip):
        start = chip * self.width
        return lax.div(start, LANES) * LANES - (start - self.halo - self.shift(chip)) - self.second

    @property
    def pad(self):
        return max(0, LANES - self.first)

    @property
    def split_length(self):
        ends = (
            self.pad + self.first - LANES + (self.n_first - 1) * TILE + WINDOW,
            self.pad + self.second - LANES + (self.n_second - 1) * TILE + WINDOW,
            self.pad + self.first + self.n_first * TILE,
            self.pad + self.length,
        )
        return ceil_to(max(ends), LANES)

    @property
    def full_length(self):
        return max(
            self.first + self.n_first * TILE, self.second + self.n_second * TILE, self.length
        )


def pack_body(ranges, bounds, chip_ref, *refs):
    chips, total, length = ranges.chips, ranges.total, ranges.length
    ins, outs = refs[:-chips], refs[-chips:]

    def cut(ref, at, lo, hi):
        pieces = []
        if lo < 0:
            pieces.append(ref[at, :, lo + total : total])
        pieces.append(ref[at, :, max(lo, 0) : min(hi, total)])
        if hi > total:
            pieces.append(ref[at, :, 0 : hi - total])
        return pieces[0] if len(pieces) == 1 else jnp.concatenate(pieces, axis=-1)

    def body(index):
        row = 0
        for ref, (low, high) in zip(ins, bounds):

            def plane(s, _, ref=ref, row=row - low, low=low):
                z = low + s * STEP
                for turn in range(chips):
                    start = ranges.starts[peer(index, turn, chips, True)]
                    value = cut(ref, pl.ds(z, STEP), start, start + length)
                    outs[turn][pl.ds(row + z, STEP)] = value
                return 0

            lax.fori_loop(0, (high - low) // STEP, plane, 0)
            row += high - low

    on_each_chip(chip_ref[0], chips, body)


def pack(ranges, chip, pieces):
    orbs = pieces[0][0].shape[1]
    bounds = [(low, high) for _, low, high in pieces]
    rows = sum(high - low for low, high in bounds)
    return call(
        functools.partial(pack_body, ranges, bounds),
        [sds(rows, orbs, ranges.length)] * ranges.chips,
        [chip, *(array for array, _, _ in pieces)],
        smem=True,
    )


def gather_body(groups, kept, chips, chip_ref, *refs):
    out = refs[-1]
    if kept:
        before = refs[0]
        out[0:kept] = before[before.shape[0] - kept :]
        refs = refs[1:]

    def body(index):
        row = kept
        for group in range(groups):
            ins = refs[group * chips : (group + 1) * chips]
            orbs = ins[0].shape[1]

            def plane(s, _, ins=ins, row=row):
                z = s * STEP
                for turn, ref in enumerate(ins):
                    slot = (peer(index, turn, chips, False) - index) % chips
                    value = ref[pl.ds(z, STEP)]
                    out[pl.ds(row + z, STEP), slot * orbs : (slot + 1) * orbs, :] = value
                return 0

            lax.fori_loop(0, ins[0].shape[0] // STEP, plane, 0)
            row += ins[0].shape[0]

    on_each_chip(chip_ref[0], chips, body)


def gather(chip, groups, before=None, kept=0):
    depth = kept + sum(g[0].shape[0] for g in groups)
    _, orbs, span = groups[0][0].shape
    chips = len(groups[0])
    return call(
        functools.partial(gather_body, len(groups), kept, chips),
        [sds(depth, orbs * chips, span)],
        [chip, *([before] if kept else []), *(p for g in groups for p in g)],
        smem=True,
    )[0]


def roll_rows(value, shift):
    if isinstance(shift, int):
        shift = shift % value.shape[1]
        if shift == 0:
            return value
    return pltpu.roll(value, shift, 1)


class Pairing:
    def __init__(self, rows, even, odd=None):
        self.rows, self.even, self.odd = rows, even, odd

    def apply(self, value, even, odd):
        if odd is None:
            return roll_rows(value, even)
        row = lax.broadcasted_iota(jnp.int32, value.shape, 1)
        return jnp.where(row % 2 == 0, roll_rows(value, even), roll_rows(value, odd))

    def negative(self, shift):
        return -shift if isinstance(shift, int) else lax.rem(self.rows - shift, self.rows)

    def partner(self, value):
        return self.apply(value, self.even, self.odd)

    def back(self, value):
        if self.odd is None:
            return self.apply(value, self.negative(self.even), None)
        return self.apply(value, self.negative(self.odd), self.negative(self.even))


def weights_body(ranges, chip_ref, out):
    i = lax.broadcasted_iota(jnp.int32, (WINDOW, TILE), 0)
    lane = lax.broadcasted_iota(jnp.int32, (1, TILE), 1)
    shift = ranges.shift(chip_ref[0])
    at = lane + LANES

    def tile(t, start, diagonal):
        y = lax.rem(lane + (start + 2 * NY) - shift, NY)
        near = (i == at - NY) | (i == at + NY)
        far = (i == at - 2 * NY) | (i == at + 2 * NY)

        def beside(step):
            wrap = jnp.where(y + step >= NY, NY, jnp.where(y + step < 0, -NY, 0))
            return i == at + step - wrap

        near = near | beside(1) | beside(-1)
        far = far | beside(2) | beside(-2)
        value = jnp.where(i == at, diagonal, 0.0)
        value = jnp.where(near, 16.0, jnp.where(far, -1.0, value))
        out[t] = value.astype(jnp.bfloat16)

    def first(t, _):
        tile(t, ranges.first + t * TILE, DIAGONAL)
        return 0

    def second(t, _):
        tile(ranges.n_first + t, ranges.second + t * TILE, 0.0)
        return 0

    lax.fori_loop(0, ranges.n_first, first, 0)
    lax.fori_loop(0, ranges.n_second, second, 0)


def weights(ranges, chip):
    shape = (ranges.n_first + ranges.n_second, WINDOW, TILE)
    out = jax.ShapeDtypeStruct(shape, jnp.bfloat16)
    return call(functools.partial(weights_body, ranges), [out], [chip], smem=True)[0]


def store_halves(ref, rows, lanes, value):
    high = value.astype(jnp.bfloat16)
    ref[0, rows, lanes] = high
    ref[1, rows, lanes] = (value - high.astype(jnp.float32)).astype(jnp.bfloat16)


def aligned(start, size):
    if isinstance(start, int):
        return slice(start, start + size)
    return pl.ds(pl.multiple_of(start, LANES), size)


def potentials(ranges, first, seconds, pairings, w_ref, work, finish):
    rho_split, rho, mid_split, mid, *products = work
    depth, n_rows, span = first.shape
    inner = depth - 2 * HALO
    swept = inner + 2 * REACH
    pad = ranges.pad
    kinds = len(seconds)

    def density(s, _):
        planes = pl.ds(s * STEP, STEP)
        rows = pl.ds(pl.multiple_of(s * (STEP * n_rows), STEP * n_rows), STEP * n_rows)
        for lo in range(0, span, LANES):
            lanes = slice(lo, lo + LANES)
            mine = first[planes, :, lanes]
            for k, (second, pairing) in enumerate(zip(seconds, pairings)):
                value = mine * pairing.partner(second[planes, :, lanes])
                value = value.reshape(STEP * n_rows, LANES)
                store_halves(rho_split.at[k], rows, slice(lo + pad, lo + pad + LANES), value)
                rho[k, rows, lanes] = value
        return 0

    lax.fori_loop(0, depth // STEP, density, 0)

    def in_plane(source, planes, start, weight, product):
        lanes = aligned(start - LANES + pad, WINDOW)
        rows = planes * n_rows
        value = source[:, :, REACH * n_rows : REACH * n_rows + rows, lanes]
        value = value.reshape(2 * kinds * rows, WINDOW)
        product[0 : 2 * kinds * rows] = jnp.dot(value, weight, preferred_element_type=jnp.float32)

    def edges(source, k, rows, start, needed):
        reach = 2 * NY - LANES
        lane = lax.broadcasted_iota(jnp.int32, (rows, LANES), 1)

        def taken(at, shift, keep):
            row = REACH * n_rows
            value = source[k, row : row + rows, aligned(at, LANES)]
            return jnp.where(keep, pltpu.roll(value, shift, 1), 0.0)

        sides = [None, None]
        if start + reach > needed[0]:
            sides[0] = taken(start - 2 * LANES, reach, lane < reach)
        if start + TILE - reach < needed[1]:
            sides[1] = taken(start + TILE + LANES, LANES - reach, lane >= LANES - reach)
        return sides

    def off(source, k, planes, start, product, needed):
        rows = planes * n_rows

        def shifted(z):
            return source[k, z * n_rows : z * n_rows + rows, aligned(start, TILE)]

        near = shifted(1) + shifted(3)
        far = shifted(0) + shifted(4)
        halves = [far[:, :LANES], far[:, LANES:]]
        for side, extra in enumerate(edges(source, k, rows, start, needed)):
            if extra is not None:
                halves[side] = halves[side] + extra
        far = jnp.concatenate(halves, axis=1)
        row = 2 * k * rows
        inside = product[row : row + rows] + product[row + rows : row + 2 * rows]
        return inside + (16.0 * near - far)

    def pipelined(count, multiply, use):
        multiply(0, products[0])
        for t in range(count):
            if t + 1 < count:
                multiply(t + 1, products[(t + 1) % 2])
            use(t, products[t % 2])

    def multiply_1(t, product):
        in_plane(rho_split, swept, ranges.first + t * TILE, w_ref[t], product)

    def use_1(t, product):
        start = ranges.first + t * TILE
        for k in range(kinds):
            value = off(rho, k, swept, start, product, ranges.needed[0])
            mid[k, :, aligned(start, TILE)] = value
            store_halves(mid_split.at[k], slice(None), aligned(start + pad, TILE), value)

    pipelined(ranges.n_first, multiply_1, use_1)

    def multiply_2(t, product):
        start = ranges.second + t * TILE
        in_plane(mid_split, inner, start, w_ref[t + ranges.n_first], product)

    def use_2(t, product):
        start = ranges.second + t * TILE
        here = aligned(start, TILE)
        values = []
        for k in range(kinds):
            value = off(mid, k, inner, start, product, ranges.needed[1])
            source = rho[k, HALO * n_rows : (HALO + inner) * n_rows, here]
            value = value + (DIAGONAL * DIAGONAL) * source
            values.append(value.reshape(inner, n_rows, TILE))
        finish(here, aligned(t * TILE, TILE), values)

    pipelined(ranges.n_second, multiply_2, use_2)


def clear(ranges, work):
    rho_split, rho, mid_split, mid = work[:4]
    span = ranges.length

    def zero(ref, lo, hi):
        if lo < hi:
            shape = ref.shape[:-1] + (hi - lo,)
            ref[..., lo:hi] = jnp.zeros(shape, ref.dtype)

    pad, end = ranges.pad, ranges.split_length
    zero(rho_split, 0, pad)
    zero(rho_split, pad + span, end)
    zero(rho, span, rho.shape[-1])
    zero(mid_split, 0, pad + ranges.first)
    zero(mid_split, pad + ranges.first + ranges.n_first * TILE, end)
    zero(mid, 0, ranges.first)
    zero(mid, ranges.first + ranges.n_first * TILE, mid.shape[-1])


def total_of(acc_in, lanes, total):
    return total if acc_in is None else (total + acc_in[:, :, lanes]) * SCALE


def same_body(ranges, follows, planes, w_ref, *refs):
    acc_in = refs[0] if follows else None
    acc, *work = refs[1:] if follows else refs
    depth, n_rows, _ = planes.shape
    inner = slice(HALO, depth - HALO)
    pairings = (Pairing(n_rows, 2), Pairing(n_rows, 1, 3))

    def finish(here, lanes, values):
        mine = planes[inner, :, here]
        total = None
        for value, pairing in zip(values, pairings):
            part = value * pairing.partner(mine) + pairing.back(value * mine)
            total = part if total is None else total + part
        acc[:, :, lanes] = total_of(acc_in, lanes, total)

    clear(ranges, work)
    potentials(ranges, planes, (planes, planes), pairings, w_ref, work, finish)


def cross_body(ranges, follows, chip_ref, planes, w_ref, other, *refs):
    acc_in = refs[0] if follows else None
    acc, travel, *work = refs[1:] if follows else refs
    depth, n_rows, _ = planes.shape
    inner = slice(HALO, depth - HALO)
    odd = chip_ref[1] == 1
    pairings = (
        Pairing(n_rows, jnp.where(odd, 0, 2)),
        Pairing(n_rows, jnp.where(odd, n_rows - 1, 1), jnp.where(odd, 1, 3)),
    )

    def finish(here, lanes, values):
        mine, theirs = planes[inner, :, here], other[inner, :, here]
        own = away = None
        for value, pairing in zip(values, pairings):
            to_own = value * pairing.partner(theirs)
            to_away = pairing.back(value * mine)
            own = to_own if own is None else own + to_own
            away = to_away if away is None else away + to_away
        acc[:, :, lanes] = total_of(acc_in, lanes, own)
        travel[:, :, lanes] = away * SCALE

    clear(ranges, work)
    potentials(ranges, planes, (other, other), pairings, w_ref, work, finish)


def split_body(ranges, chip_ref, mine, theirs, *outs):
    orbs = outs[0].shape[1]
    lanes = aligned(ranges.out_at(chip_ref[0]), ranges.out_length)

    def body(index):
        def plane(s, _):
            at = pl.ds(s * STEP, STEP)
            value = mine[at, :, lanes] + theirs[at, :, lanes]
            for turn, out in enumerate(outs):
                slot = (peer(index, turn, ranges.chips, True) - index) % ranges.chips
                out[at] = value[:, slot * orbs : (slot + 1) * orbs]
            return 0

        lax.fori_loop(0, outs[0].shape[0] // STEP, plane, 0)

    on_each_chip(chip_ref[0], ranges.chips, body)


def place_body(ranges, chip_ref, *refs):
    chips = ranges.chips
    ins, out = refs[:-1], refs[-1]

    def body(index):
        row = 0
        for first in range(0, len(ins), chips):

            def plane(s, _, row=row, first=first):
                at = pl.ds(s * STEP, STEP)
                into = pl.ds(row + s * STEP, STEP)
                for turn in range(chips):
                    source = peer(index, turn, chips, False)
                    base = ranges.out_starts[source]
                    lane, hi = source * ranges.width, (source + 1) * ranges.width
                    while lane < hi:
                        stop = min(floor_to(lane, LANES) + LANES, hi)
                        if lane % LANES == 0:
                            stop = max(floor_to(hi, LANES), stop)
                        out[into, :, lane:stop] = ins[first + turn][at, :, lane - base : stop - base]
                        lane = stop
                return 0

            lax.fori_loop(0, ins[first].shape[0] // STEP, plane, 0)
            row += ins[first].shape[0]

    on_each_chip(chip_ref[0], chips, body)


def per_device(n_band, orbitals):
    orbs, depth, total = orbitals.shape
    chips = n_band // 2
    ranges = Ranges(chips, total)
    index = lax.axis_index("band")
    chip = jnp.stack([index // 2, index % 2]).astype(jnp.int32)
    planes = jnp.transpose(orbitals, (1, 0, 2))

    def exchange(value, turn):
        pairs = [(i, peer(i // 2, turn, chips, True) * 2 + i % 2) for i in range(n_band)]
        return lax.ppermute(value, "band", pairs)

    def partner_core(value):
        return lax.ppermute(value, "band", [(i, i ^ 1) for i in range(n_band)])

    n_slab = lax.axis_size("slab")
    up = [(i, (i + 1) % n_slab) for i in range(n_slab)]
    down = [(j, i) for i, j in up]
    below = lax.ppermute(planes[depth - HALO :], "slab", up)
    above = lax.ppermute(planes[:HALO], "slab", down)

    def spread(sent):
        got = [sent[0]]
        for turn in range(1, chips):
            got.append(exchange(sent[turn], turn))
        return got

    def fetch(pieces):
        sent = pack(ranges, chip, pieces)
        return spread(sent)

    inner = depth // CHUNKS
    cut = inner + HALO
    got_a = fetch([(planes, 0, cut)])
    banded = weights(ranges, chip)
    got_low = fetch([(below, 0, HALO)])
    got_b = fetch([(planes, cut, depth), (above, 0, HALO)])
    planes_a = gather(chip, [got_low, got_a])

    rows = orbs * chips
    full, swept = (inner + 2 * HALO) * rows, (inner + 2 * REACH) * rows
    work = [
        pltpu.VMEM((2, 2, full, ranges.split_length), jnp.bfloat16),
        pltpu.VMEM((2, full, ranges.full_length), jnp.float32),
        pltpu.VMEM((2, 2, swept, ranges.split_length), jnp.bfloat16),
        pltpu.VMEM((2, swept, ranges.full_length), jnp.float32),
        pltpu.VMEM((4 * swept, TILE), jnp.float32),
        pltpu.VMEM((4 * swept, TILE), jnp.float32),
    ]
    result = sds(inner, rows, ranges.n_second * TILE)
    flops = 8 * WINDOW * TILE * (ranges.n_first + ranges.n_second) * full

    def same(mine, *acc):
        return call(
            functools.partial(same_body, ranges, bool(acc)),
            [result],
            [mine, banded, *acc],
            scratch=work,
            flops=flops,
            limit=12 + 12 * (rows // 8),
        )[0]

    def cross(mine, other, *acc):
        own, travel = call(
            functools.partial(cross_body, ranges, bool(acc)),
            [result, result],
            [chip, mine, banded, other, *acc],
            scratch=work,
            flops=flops,
            smem=True,
            limit=12 + 12 * (rows // 8),
        )
        return own, partner_core(travel)

    def give(acc, back):
        parts = call(
            functools.partial(split_body, ranges),
            [sds(inner, orbs, ranges.out_length)] * chips,
            [chip, acc, back],
            smem=True,
        )
        return spread(parts)

    other_a = partner_core(planes_a)
    acc_a = same(planes_a)
    acc_a, back_a = cross(planes_a, other_a, acc_a)
    planes_b = gather(chip, [got_b], before=planes_a, kept=2 * HALO)
    other_b = partner_core(planes_b)
    home = give(acc_a, back_a)
    acc_b, back_b = cross(planes_b, other_b)
    acc_b = same(planes_b, acc_b)
    home += give(acc_b, back_b)
    out = call(
        functools.partial(place_body, ranges), [sds(depth, orbs, total)], [chip, *home], smem=True
    )[0]
    return jnp.transpose(out, (1, 0, 2))


def solution(mesh):
    def body(orbitals):
        return per_device(mesh.shape["band"], orbitals)

    return jax.shard_map(
        body,
        mesh=mesh,
        in_specs=(P("band", "slab", None),),
        out_specs=P("band", "slab", None),
        check_vma=False,
    )
```
